512 devices in a mesh: blk: 32 (over x_hi, z, core), adp: 16 (over y, x_lo).
Axes of the slice: x: 4 (x_hi: 2, x_lo: 2; x = x_hi * 2 + x_lo), y: 8, z: 8, core: 2. Of those that a mesh axis runs over, the one named last changes fastest.
Arguments:
- stream: bfloat16 [16384, 1536], P(('blk', 'adp')), may hold values from -6 to 6
- prenorm_gain: float32 [1536], replicated, may hold values from 0.25 to 1.75
- gate_up_weight: bfloat16 [2, 4608, 1536], P(None, 'blk'), may hold values from -0.15625 to 0.15625
- down_weight: bfloat16 [4608, 1536], P('blk'), may hold values from -0.09375 to 0.09375
- adapter_gate_input: bfloat16 [64, 32, 1536], P('adp'), may hold values from -0.15625 to 0.15625
- adapter_gate_output: bfloat16 [64, 2, 16, 4608], P('adp', None, None, 'blk'), may hold values from -0.75 to 0.75
- adapter_down_input: bfloat16 [64, 4608, 16], P('adp', 'blk'), may hold values from -0.09375 to 0.09375
- adapter_down_output: bfloat16 [64, 16, 1536], P('adp'), may hold values from -0.75 to 0.75
- adapter_of_request: int32 [256], replicated, may hold values from 0 to 63, as said below
- request_of_slot: int32 [16384], P(('blk', 'adp')), may hold values from 0 to 255
Outputs:
- mixed: bfloat16 [16384, 1536], P(('blk', 'adp'))
The draws below stay inside these ranges and needn't reach their ends.
Inputs may be any that keep to these rules, and one draw needn't show every extreme that they name: `adapter_of_request`: exactly 16 distinct adapter numbers occur.
All inputs are finite; a program needn't handle non-finite values.
Results may differ from the reference program's by a relative error of at most 0.014.
Values may be sent and summed in bfloat16 or wider, within the bound.
A program may use at most 64 MiB of HBM per device.

```python
import jax
import jax.numpy as jnp
from jax import lax

MODEL_WIDTH = 1536
HIDDEN_UNITS = 4608
ADAPTER_RANK = 16
TOK_DEV = 32
ACTIVE = 16
REQUESTS = 256
ADAPTER_TOTAL = 64
TOKENS = 16384
N_BLK = 32


def draw_adapter_of_request(key, part):
    key_pick = jax.random.fold_in(key, 11)
    key_first = jax.random.fold_in(key, 12)
    key_second = jax.random.fold_in(key, 13)
    key_order = jax.random.fold_in(key, 14)
    middle = 1 + jax.random.permutation(key_pick, ADAPTER_TOTAL - 2)[:ACTIVE - 2]
    ends = jnp.array([0, ADAPTER_TOTAL - 1], dtype=jnp.int32)
    joined = jnp.concatenate([ends, middle.astype(jnp.int32)])
    chosen = joined[jax.random.permutation(key_order, ACTIVE)]
    first = jax.random.randint(key_first, (REQUESTS,), 0, ACTIVE)
    second = jax.random.randint(key_second, (REQUESTS,), 0, ACTIVE)
    picked = jnp.minimum(first, second)
    counter = jnp.arange(REQUESTS)
    picked = jnp.where(counter < ACTIVE, counter, picked)
    return chosen[picked].astype(jnp.int32)


def with_ends(values, own_key, smallest, high):
    dims = values.shape
    index_at = [jax.random.randint(jax.random.fold_in(own_key, axis), (), 0, dims[axis]) for axis in range(len(dims))]
    values = values.at[tuple(index_at)].set(smallest)
    longest = dims.index(max(dims))
    index_at[longest] = (index_at[longest] + 1) % dims[longest]
    return values.at[tuple(index_at)].set(high)


def shard_levels(stream_key, extent, pieces, low, largest):
    level = 1.0
    for axis_at, blocks in pieces:
        draws = jax.random.uniform(jax.random.fold_in(jax.random.fold_in(stream_key, 6), axis_at), (blocks,), jnp.float32, low / len(pieces), largest / len(pieces))
        level = level * jnp.repeat(jnp.exp(draws), extent[axis_at] // blocks).reshape((-1,) + (1,) * (len(extent) - 1 - axis_at))
    return level


def noise(rng, dims, width, reach, shards=(), kind=jnp.bfloat16):
    values = jax.random.normal(rng, dims, jnp.float32) * width
    if len(shards) > 0:
        values = shard_levels(rng, dims, shards, -0.22, 0.18) * values
    return jnp.clip(values, min=-reach, max=reach).astype(kind)


def setup_inputs(seed: int = 0) -> dict:
    keys = jax.random.split(jax.random.key(seed), 11)
    return {
        "stream": noise(keys[0], (TOKENS, MODEL_WIDTH), 1.0, 6.0, ((0, 512),)),
        "prenorm_gain": jnp.clip(1.0 + 0.15 * jax.random.normal(keys[1], (MODEL_WIDTH,), jnp.float32), 0.25, 1.75),
        "gate_up_weight": noise(keys[2], (2, HIDDEN_UNITS, MODEL_WIDTH), MODEL_WIDTH ** -0.5, 0.15625, ((1, 32),)),
        "down_weight": noise(keys[3], (HIDDEN_UNITS, MODEL_WIDTH), HIDDEN_UNITS ** -0.5, 0.09375, ((0, 32),)),
        "adapter_gate_input": noise(keys[4], (ADAPTER_TOTAL, 2 * ADAPTER_RANK, MODEL_WIDTH), MODEL_WIDTH ** -0.5, 0.15625, ((0, 16),)),
        "adapter_gate_output": noise(keys[5], (ADAPTER_TOTAL, 2, ADAPTER_RANK, HIDDEN_UNITS), (4 * ADAPTER_RANK) ** -0.5, 0.75, ((0, 16), (3, 32))),
        "adapter_down_input": noise(keys[6], (ADAPTER_TOTAL, HIDDEN_UNITS, ADAPTER_RANK), HIDDEN_UNITS ** -0.5, 0.09375, ((0, 16), (1, 32))),
        "adapter_down_output": noise(keys[7], (ADAPTER_TOTAL, ADAPTER_RANK, MODEL_WIDTH), (4 * ADAPTER_RANK) ** -0.5, 0.75, ((0, 16),)),
        "adapter_of_request": draw_adapter_of_request(jax.random.fold_in(keys[10], 71), 0),
        "request_of_slot": with_ends(jax.random.randint(keys[9], (TOKENS,), 0, REQUESTS), jax.random.fold_in(keys[9], 1), 0, REQUESTS - 1).astype(jnp.int32),
    }


def reference(stream, prenorm_gain, gate_up_weight, down_weight, adapter_gate_input, adapter_gate_output, adapter_down_input, adapter_down_output, adapter_of_request, request_of_slot):
    adapter = adapter_of_request[request_of_slot].astype(jnp.int32)
    blocks = TOKENS // TOK_DEV
    hidden_dev = HIDDEN_UNITS // N_BLK
    gate_up = gate_up_weight.reshape(2 * HIDDEN_UNITS, MODEL_WIDTH)
    down_split = down_weight.astype(jnp.float32).reshape(N_BLK, hidden_dev, MODEL_WIDTH)

    def one_block(couple):
        rows, adapter_index = couple
        value_rows = rows.astype(jnp.float32)
        scale = lax.rsqrt(lax.optimization_barrier(jnp.mean(value_rows * value_rows, axis=-1, keepdims=True)) + 1e-06)
        normed = (value_rows * scale * prenorm_gain).astype(jnp.bfloat16)
        input_factor = adapter_gate_input[adapter_index].astype(jnp.float32)
        lowrank_input = jnp.einsum('td,trd->tr', normed.astype(jnp.float32), input_factor).astype(jnp.bfloat16)
        base_output = lax.dot_general(normed, gate_up, (((1,), (1,)), ((), ())), preferred_element_type=jnp.float32).reshape(-1, 2, HIDDEN_UNITS)
        output_factor = adapter_gate_output[adapter_index].astype(jnp.float32)
        adapter_delta = jnp.einsum('vau,vauj->vaj', lowrank_input.astype(jnp.float32).reshape(-1, 2, ADAPTER_RANK), output_factor)
        prenorm_input = base_output + adapter_delta
        hidden = (jax.nn.gelu(prenorm_input[:, 0], approximate=True) * prenorm_input[:, 1]).astype(jnp.bfloat16)
        parts = jnp.einsum('tkf,kfd->tkd', hidden.astype(jnp.float32).reshape(-1, N_BLK, hidden_dev), down_split)
        parts = lax.optimization_barrier(parts.astype(jnp.bfloat16)).astype(jnp.float32)
        down_total = lax.optimization_barrier(jnp.sum(parts, axis=1))
        down_input_factor = adapter_down_input[adapter_index].astype(jnp.float32)
        lowrank_down = jnp.einsum('tf,tfr->tr', hidden.astype(jnp.float32), down_input_factor).astype(jnp.bfloat16)
        down_output_factor = adapter_down_output[adapter_index].astype(jnp.float32)
        adapter_output = jnp.einsum('pm,pmy->py', lowrank_down.astype(jnp.float32), down_output_factor)
        return (value_rows + down_total + adapter_output).astype(jnp.bfloat16)
    mixed = lax.map(one_block, (stream.reshape(blocks, TOK_DEV, MODEL_WIDTH), adapter.reshape(blocks, TOK_DEV)))
    return mixed.reshape(TOKENS, MODEL_WIDTH)
```

```python
import jax
import jax.numpy as jnp
from jax import lax
from jax.sharding import PartitionSpec as P

ACTIVE = 16


norm_eps = 1e-06


def normalize(rows, gain):
    value_rows = rows.astype(jnp.float32)
    scale = lax.rsqrt(jnp.mean(value_rows * value_rows, axis=-1, keepdims=True) + norm_eps)
    return (value_rows * scale * gain).astype(jnp.bfloat16)


def local(
    stream,
    prenorm_gain,
    gate_up_weight,
    down_weight,
    adapter_gate_input,
    adapter_gate_output,
    adapter_down_input,
    adapter_down_output,
    adapter_of_request,
    request_of_slot,
):
    width = stream.shape[1]
    tok_rows = stream.shape[0]
    hidden_dev = down_weight.shape[0]
    rank_columns = adapter_down_output.shape[1]
    holders = lax.axis_size("adp")
    kept_rows = adapter_gate_input.shape[0]
    catalog = jnp.arange(kept_rows * holders, dtype=jnp.int32)
    used = jnp.any(adapter_of_request[:, None] == catalog[None, :], axis=0)
    order = jnp.cumsum(used.astype(jnp.int32)) - 1
    active_pos = jnp.arange(ACTIVE, dtype=jnp.int32)
    picked = used[None, :] & (order[None, :] == active_pos[:, None])
    active = jnp.sum(jnp.where(picked, catalog[None, :], 0), axis=1)
    every = (
        lax.all_gather(adapter_gate_input, "adp", axis=0, tiled=True),
        lax.all_gather(adapter_gate_output, "adp", axis=0, tiled=True),
        lax.all_gather(adapter_down_input, "adp", axis=0, tiled=True),
        lax.all_gather(adapter_down_output, "adp", axis=0, tiled=True),
    )
    input_factor = jnp.take(every[0], active, axis=0)
    output_factor = jnp.take(every[1], active, axis=0)
    down_input_factor = jnp.take(every[2], active, axis=0)
    down_output_factor = jnp.take(every[3], active, axis=0)
    table = jnp.arange(adapter_of_request.shape[0], dtype=jnp.int32)
    own_adapter = jnp.sum(
        jnp.where(request_of_slot[:, None] == table[None, :], adapter_of_request[None, :], 0),
        axis=1,
    )
    own_match = own_adapter[:, None] == active[None, :]
    own_slot = jnp.sum(jnp.where(own_match, active_pos[None, :], 0), axis=1)
    normed = normalize(stream, prenorm_gain)
    packed = jnp.concatenate(
        [normed, jnp.broadcast_to(own_slot.astype(jnp.bfloat16)[:, None], (tok_rows, 128))], axis=1
    )
    gathered = lax.all_gather(packed, "blk", axis=0, tiled=True)
    all_rows = gathered[:, :width]
    group_match = gathered[:, width : width + 1].astype(jnp.float32) == active_pos.astype(
        jnp.float32
    )
    match_ranks = jnp.repeat(group_match, rank_columns, axis=1)
    cat_rows = ACTIVE * rank_columns

    pre = []
    for side in range(2):
        rows_in = input_factor[:, side * rank_columns : (side + 1) * rank_columns]
        low = lax.dot_general(
            all_rows,
            rows_in.reshape(cat_rows, width),
            (((1,), (1,)), ((), ())),
            preferred_element_type=jnp.float32,
        )
        low_spread = jnp.where(match_ranks, low, 0).astype(jnp.bfloat16)
        base = lax.dot_general(
            all_rows,
            gate_up_weight[side],
            (((1,), (1,)), ((), ())),
            preferred_element_type=jnp.float32,
        )
        pre.append(
            base
            + jnp.dot(
                low_spread,
                output_factor[:, side].reshape(cat_rows, hidden_dev),
                preferred_element_type=jnp.float32,
            )
        )
    hidden = (jax.nn.gelu(pre[0], approximate=True) * pre[1]).astype(jnp.bfloat16)
    down_in = down_input_factor.transpose(1, 0, 2).reshape(hidden_dev, cat_rows)
    partial_value = jnp.dot(hidden, down_in, preferred_element_type=jnp.float32)
    low_spread = jnp.where(match_ranks, partial_value, 0).astype(jnp.bfloat16)
    part = jnp.dot(hidden, down_weight, preferred_element_type=jnp.float32) + jnp.dot(
        low_spread,
        down_output_factor.reshape(cat_rows, width),
        preferred_element_type=jnp.float32,
    )
    total = lax.psum_scatter(
        part.astype(jnp.bfloat16), "blk", scatter_dimension=0, tiled=True
    ).astype(jnp.float32)
    return (stream.astype(jnp.float32) + total).astype(jnp.bfloat16)


def solution(mesh):
    in_specs = (
        P(("blk", "adp"), None),
        P(),
        P(None, "blk", None),
        P("blk", None),
        P("adp", None, None),
        P("adp", None, None, "blk"),
        P("adp", "blk", None),
        P("adp", None, None),
        P(),
        P(("blk", "adp")),
    )
    out_specs = P(("blk", "adp"), None)
    return jax.shard_map(local, mesh=mesh, in_specs=in_specs, out_specs=out_specs, check_vma=False)
```

```python
import jax
import jax.numpy as jnp
from jax import lax
from jax.experimental import pallas as pl
from jax.experimental.pallas import tpu as pltpu
from jax.sharding import PartitionSpec as P

ACTIVE = 16
RING = 8
FWD, BWD = 0, 1
OWN, OTHER = 0, 1

norm_eps = 1e-06


def normalize(rows, gain):
    value_rows = rows.astype(jnp.float32)
    scale = lax.rsqrt(jnp.mean(value_rows * value_rows, axis=-1, keepdims=True) + norm_eps)
    return (value_rows * scale * gain).astype(jnp.bfloat16)


def blk_index(x_hi, z, core):
    return x_hi * (2 * RING) + z * 2 + core


def greet(targets):
    barrier = pltpu.get_barrier_semaphore()
    for target in targets:
        pl.semaphore_signal(
            barrier, inc=1, device_id=target, device_id_type=pl.DeviceIdType.MESH
        )
    pl.semaphore_wait(barrier, len(targets))


def remote(src, dst, send_sem, recv_sem, target):
    return pltpu.make_async_remote_copy(
        src_ref=src,
        dst_ref=dst,
        send_sem=send_sem,
        recv_sem=recv_sem,
        device_id=target,
        device_id_type=pl.DeviceIdType.MESH,
    )


def adp_peers(holders):
    me = lax.axis_index("adp")
    return [{"adp": lax.rem(me + step, holders)} for step in range(1, holders)]


def adp_start(holders, own_ref, all_ref, send_sem, recv_sem):
    me = lax.axis_index("adp")
    copies = []
    for step, target in enumerate(adp_peers(holders)):
        copy = remote(own_ref, all_ref.at[me], send_sem.at[step], recv_sem.at[step], target)
        copy.start()
        copies.append(copy)
    return copies


def adp_finish(holders, copies, all_ref, recv_sem, send_sem):
    me = lax.axis_index("adp")
    for step, target in enumerate(adp_peers(holders)):
        source = lax.rem(me + holders - step - 1, holders)
        slab = all_ref.at[source]
        remote(slab, slab, send_sem.at[step], recv_sem.at[step], target).wait_recv()
    for copy in copies:
        copy.wait_send()


def adp_gather_kernel(holders, own_ref, all_ref, send_sem, recv_sem, local_sem):
    me = lax.axis_index("adp")
    greet(adp_peers(holders))
    copies = adp_start(holders, own_ref, all_ref, send_sem, recv_sem)
    keep = pltpu.make_async_copy(own_ref, all_ref.at[me], local_sem)
    keep.start()
    adp_finish(holders, copies, all_ref, recv_sem, send_sem)
    keep.wait()


def adp_gather(own, holders):
    def kernel(*refs):
        adp_gather_kernel(holders, *refs)

    return pl.pallas_call(
        kernel,
        out_shape=jax.ShapeDtypeStruct((holders,) + own.shape, own.dtype),
        in_specs=[pl.BlockSpec(memory_space=pltpu.VMEM)],
        out_specs=pl.BlockSpec(memory_space=pltpu.VMEM),
        scratch_shapes=[
            pltpu.SemaphoreType.DMA((holders - 1,)),
            pltpu.SemaphoreType.DMA((holders - 1,)),
            pltpu.SemaphoreType.DMA,
        ],
        compiler_params=pltpu.CompilerParams(collective_id=1, has_side_effects=True),
        name="adp_gather",
    )(own)


def reach(stream, way):
    return 4 if (stream == OWN) == (way == FWD) else 3


def rows_gather(own, factors, holders):
    blocks = 4 * RING

    def kernel(
        own_ref,
        factor_ref,
        all_ref,
        factor_all_ref,
        ring_send,
        ring_recv,
        across_send,
        across_recv,
        sib_send,
        sib_recv,
        adp_send,
        adp_recv,
        local_sem,
    ):
        me = lax.axis_index("blk")
        me_adp = lax.axis_index("adp")
        x_hi = me // (2 * RING)
        z = lax.rem(me // 2, RING)
        core = lax.rem(me, 2)
        sibling = {"blk": blk_index(x_hi, z, 1 - core)}
        across = {"blk": blk_index(1 - x_hi, z, core)}
        ahead = {
            FWD: {"blk": blk_index(x_hi, lax.rem(z + 1, RING), core)},
            BWD: {"blk": blk_index(x_hi, lax.rem(z + RING - 1, RING), core)},
        }
        greet([sibling, across, ahead[FWD], ahead[BWD]] + adp_peers(holders))
        sent = []

        def at(stream, way, far, owner_core):
            x_of = x_hi if stream == OWN else 1 - x_hi
            z_of = lax.rem(z + RING - far, RING) if way == FWD else lax.rem(z + far, RING)
            return blk_index(x_of, z_of, owner_core)

        def push(src, index, send_sem, recv_sem, target):
            copy = remote(src, all_ref.at[index], send_sem, recv_sem, target)
            copy.start()
            sent.append(copy)

        def to_ring(src, index, stream, way, far):
            push(
                src,
                index,
                ring_send.at[stream, way, far],
                ring_recv.at[stream, way, far],
                ahead[way],
            )

        def to_sibling(src, index, stream, way, far):
            push(
                src,
                index,
                sib_send.at[stream, way, far],
                sib_recv.at[stream, way, far],
                sibling,
            )

        push(own_ref, me, across_send, across_recv, across)
        to_ring(own_ref, me, OWN, FWD, 0)
        to_ring(own_ref, me, OWN, BWD, 0)
        to_sibling(own_ref, me, OWN, FWD, 0)
        adp_copies = adp_start(holders, factor_ref, factor_all_ref, adp_send, adp_recv)
        keep = pltpu.make_async_copy(own_ref, all_ref.at[me], local_sem.at[0])
        keep.start()
        keep_factor = pltpu.make_async_copy(factor_ref, factor_all_ref.at[me_adp], local_sem.at[1])
        keep_factor.start()

        other = at(OTHER, FWD, 0, core)
        slab = all_ref.at[other]
        remote(slab, slab, across_send, across_recv, across).wait_recv()
        to_ring(slab, other, OTHER, FWD, 0)
        to_ring(slab, other, OTHER, BWD, 0)
        to_sibling(slab, other, OTHER, FWD, 0)
        for far in range(1, 5):
            for stream in (OWN, OTHER):
                for way in (FWD, BWD):
                    last = reach(stream, way)
                    if far > last:
                        continue
                    index = at(stream, way, far, core)
                    slab = all_ref.at[index]
                    remote(
                        slab,
                        slab,
                        ring_send.at[stream, way, far - 1],
                        ring_recv.at[stream, way, far - 1],
                        ahead[way],
                    ).wait_recv()
                    if far < last:
                        to_ring(slab, index, stream, way, far)
                    to_sibling(slab, index, stream, way, far)
        for far in range(0, 5):
            for stream in (OWN, OTHER):
                for way in (FWD, BWD):
                    if far > reach(stream, way) or (far == 0 and way == BWD):
                        continue
                    slab = all_ref.at[at(stream, way, far, 1 - core)]
                    remote(
                        slab,
                        slab,
                        sib_send.at[stream, way, far],
                        sib_recv.at[stream, way, far],
                        sibling,
                    ).wait_recv()
        adp_finish(holders, adp_copies, factor_all_ref, adp_recv, adp_send)
        for copy in sent:
            copy.wait_send()
        keep.wait()
        keep_factor.wait()

    dma = pltpu.SemaphoreType.DMA
    return pl.pallas_call(
        kernel,
        out_shape=[
            jax.ShapeDtypeStruct((blocks,) + own.shape, own.dtype),
            jax.ShapeDtypeStruct((holders,) + factors.shape, factors.dtype),
        ],
        in_specs=[pl.BlockSpec(memory_space=pltpu.VMEM)] * 2,
        out_specs=[pl.BlockSpec(memory_space=pltpu.VMEM)] * 2,
        scratch_shapes=[
            dma((2, 2, 4)),
            dma((2, 2, 4)),
            dma,
            dma,
            dma((2, 2, 5)),
            dma((2, 2, 5)),
            dma((holders - 1,)),
            dma((holders - 1,)),
            dma((2,)),
        ],
        compiler_params=pltpu.CompilerParams(collective_id=2, has_side_effects=True),
        name="rows_gather",
    )(own, factors)


def sum_scatter(parts):
    rows, width = parts.shape[1:]

    def kernel(
        part_ref,
        out_ref,
        sib_ref,
        leave_ref,
        arrive_ref,
        cross_out_ref,
        cross_in_ref,
        ring_send,
        ring_recv,
        across_send,
        across_recv,
        sib_send,
        sib_recv,
    ):
        me = lax.axis_index("blk")
        x_hi = me // (2 * RING)
        z = lax.rem(me // 2, RING)
        core = lax.rem(me, 2)
        sibling = {"blk": blk_index(x_hi, z, 1 - core)}
        across = {"blk": blk_index(1 - x_hi, z, core)}
        ahead = {
            FWD: {"blk": blk_index(x_hi, lax.rem(z + 1, RING), core)},
            BWD: {"blk": blk_index(x_hi, lax.rem(z + RING - 1, RING), core)},
        }
        greet([sibling, across, ahead[FWD], ahead[BWD]])
        sent = []

        def at(stream, way, far, owner_core):
            x_of = x_hi if stream == OWN else 1 - x_hi
            z_of = lax.rem(z + far, RING) if way == FWD else lax.rem(z + RING - far, RING)
            return blk_index(x_of, z_of, owner_core)

        def push(copy):
            copy.start()
            sent.append(copy)

        order = []
        for far in range(4, -1, -1):
            for stream in (OTHER, OWN):
                for way in (FWD, BWD):
                    if far <= reach(stream, way) and not (far == 0 and way == BWD):
                        order.append((stream, way, far))

        def sib_copy(stream, way, far):
            return remote(
                part_ref.at[at(stream, way, far, 1 - core)],
                sib_ref.at[stream, way, far],
                sib_send.at[stream, way, far],
                sib_recv.at[stream, way, far],
                sibling,
            )

        for key in order:
            push(sib_copy(*key))

        def pair_sum(stream, way, far):
            sib_copy(stream, way, far).wait_recv()
            own = part_ref[at(stream, way, far, core)].astype(jnp.float32)
            return own + sib_ref[stream, way, far].astype(jnp.float32)

        def ring_copy(stream, way, far):
            return remote(
                leave_ref.at[stream, way, far - 1],
                arrive_ref.at[stream, way, far - 1],
                ring_send.at[stream, way, far - 1],
                ring_recv.at[stream, way, far - 1],
                ahead[way],
            )

        def arrived(stream, way, far):
            ring_copy(stream, way, far + 1).wait_recv()
            return arrive_ref[stream, way, far].astype(jnp.float32)

        totals = {}
        for key in order:
            stream, way, far = key
            total = pair_sum(*key)
            if far == 0:
                total = total + arrived(stream, FWD, 0) + arrived(stream, BWD, 0)
                if stream == OTHER:
                    cross_out_ref[...] = total.astype(cross_out_ref.dtype)
                    push(remote(cross_out_ref, cross_in_ref, across_send, across_recv, across))
                else:
                    totals[stream] = total
                continue
            if far < reach(stream, way):
                total = total + arrived(stream, way, far)
            leave_ref[stream, way, far - 1] = total.astype(leave_ref.dtype)
            push(ring_copy(stream, way, far))
        remote(cross_out_ref, cross_in_ref, across_send, across_recv, across).wait_recv()
        out_ref[...] = totals[OWN] + cross_in_ref[...].astype(jnp.float32)
        for copy in sent:
            copy.wait_send()

    dma = pltpu.SemaphoreType.DMA
    block = (rows, width)
    return pl.pallas_call(
        kernel,
        out_shape=jax.ShapeDtypeStruct(block, jnp.float32),
        in_specs=[pl.BlockSpec(memory_space=pltpu.VMEM)],
        out_specs=pl.BlockSpec(memory_space=pltpu.VMEM),
        scratch_shapes=[
            pltpu.VMEM((2, 2, 5) + block, parts.dtype),
            pltpu.VMEM((2, 2, 4) + block, parts.dtype),
            pltpu.VMEM((2, 2, 4) + block, parts.dtype),
            pltpu.VMEM(block, parts.dtype),
            pltpu.VMEM(block, parts.dtype),
            dma((2, 2, 4)),
            dma((2, 2, 4)),
            dma,
            dma,
            dma((2, 2, 5)),
            dma((2, 2, 5)),
        ],
        compiler_params=pltpu.CompilerParams(collective_id=3, has_side_effects=True),
        name="sum_scatter",
    )(parts)


def local(
    stream,
    prenorm_gain,
    gate_up_weight,
    down_weight,
    adapter_gate_input,
    adapter_gate_output,
    adapter_down_input,
    adapter_down_output,
    adapter_of_request,
    request_of_slot,
):
    width = stream.shape[1]
    tok_rows = stream.shape[0]
    hidden_dev = down_weight.shape[0]
    rank_columns = adapter_down_output.shape[1]
    holders = lax.axis_size("adp")
    kept_rows = adapter_gate_input.shape[0]
    catalog = jnp.arange(kept_rows * holders, dtype=jnp.int32)
    used = jnp.any(adapter_of_request[:, None] == catalog[None, :], axis=0)
    order = jnp.cumsum(used.astype(jnp.int32)) - 1
    active_pos = jnp.arange(ACTIVE, dtype=jnp.int32)
    picked = used[None, :] & (order[None, :] == active_pos[:, None])
    active = jnp.sum(jnp.where(picked, catalog[None, :], 0), axis=1)
    table = jnp.arange(adapter_of_request.shape[0], dtype=jnp.int32)
    own_adapter = jnp.sum(
        jnp.where(request_of_slot[:, None] == table[None, :], adapter_of_request[None, :], 0),
        axis=1,
    )
    own_match = own_adapter[:, None] == active[None, :]
    own_slot = jnp.sum(jnp.where(own_match, active_pos[None, :], 0), axis=1)
    normed = normalize(stream, prenorm_gain)
    place = lax.axis_index("blk")
    half = width // 2
    row_in = lax.dynamic_slice_in_dim(adapter_gate_input, place, 1, axis=1)[:, 0]
    row_out = lax.dynamic_slice(
        adapter_down_output, (0, place // 2, lax.rem(place, 2) * half), (kept_rows, 1, half)
    )[:, 0]
    catalog_rows = adp_gather(jnp.concatenate([row_in, row_out], axis=1), holders)
    choose = (active[:, None] == catalog[None, :]).astype(jnp.bfloat16)
    chosen = jnp.dot(
        choose, catalog_rows.reshape(-1, width + half), preferred_element_type=jnp.float32
    ).astype(jnp.bfloat16)
    tile_cols = half // 3
    packed = jnp.concatenate(
        [
            jnp.concatenate([normed, chosen[:, :width]], axis=0),
            jnp.concatenate(
                [chosen[:, width + k * tile_cols : width + (k + 1) * tile_cols] for k in range(3)],
                axis=0,
            ),
            jnp.concatenate(
                [
                    jnp.broadcast_to(own_slot.astype(jnp.bfloat16)[:, None], (tok_rows, 128)),
                    jnp.zeros((ACTIVE, 128), jnp.bfloat16),
                ],
                axis=0,
            ),
        ],
        axis=1,
    )
    own_factors = jnp.concatenate(
        [
            adapter_gate_output.reshape(kept_rows, 2 * rank_columns, hidden_dev),
            adapter_down_input.transpose(0, 2, 1),
        ],
        axis=1,
    )
    gathered, factors = rows_gather(packed, own_factors, holders)
    factors = jnp.take(
        factors.reshape(kept_rows * holders, 3 * rank_columns, hidden_dev), active, axis=0
    ).transpose(1, 0, 2)
    cat_rows = ACTIVE * rank_columns
    factors = factors.reshape(3, cat_rows, hidden_dev)
    all_rows = gathered[:, :tok_rows, :width].reshape(-1, width)
    rows_in = gathered[:, tok_rows:, :width].reshape(2, cat_rows, width)
    down_out = (
        gathered[:, :, width : width + tile_cols]
        .reshape(rank_columns, 2, 3, ACTIVE, tile_cols)
        .transpose(0, 3, 1, 2, 4)
        .reshape(cat_rows, width)
    )
    all_slot = gathered[:, :tok_rows, width + tile_cols].reshape(-1, 1).astype(jnp.int32)
    match = all_slot == (jnp.arange(cat_rows, dtype=jnp.int32) % ACTIVE)[None, :]
    contract_minor = (((1,), (1,)), ((), ()))
    pre = []
    for side in range(2):
        low = lax.dot_general(
            all_rows, rows_in[side], contract_minor, preferred_element_type=jnp.float32
        )
        base = lax.dot_general(
            all_rows, gate_up_weight[side], contract_minor, preferred_element_type=jnp.float32
        )
        low_spread = jnp.where(match, low, 0).astype(jnp.bfloat16)
        pre.append(base + jnp.dot(low_spread, factors[side], preferred_element_type=jnp.float32))
    hidden = (jax.nn.gelu(pre[0], approximate=True) * pre[1]).astype(jnp.bfloat16)
    low_part = lax.dot_general(
        hidden, factors[2], contract_minor, preferred_element_type=jnp.float32
    )
    low_spread = jnp.where(match, low_part, 0).astype(jnp.bfloat16)
    part = jnp.dot(hidden, down_weight, preferred_element_type=jnp.float32) + jnp.dot(
        low_spread, down_out, preferred_element_type=jnp.float32
    )
    total = sum_scatter(part.astype(jnp.bfloat16).reshape(-1, tok_rows, width))
    return (stream.astype(jnp.float32) + total).astype(jnp.bfloat16)


def solution(mesh):
    in_specs = (
        P(("blk", "adp"), None),
        P(),
        P(None, "blk", None),
        P("blk", None),
        P("adp", None, None),
        P("adp", None, None, "blk"),
        P("adp", "blk", None),
        P("adp", None, None),
        P(),
        P(("blk", "adp")),
    )
    out_specs = P(("blk", "adp"), None)
    return jax.shard_map(local, mesh=mesh, in_specs=in_specs, out_specs=out_specs, check_vma=False)
```

```python
import jax
import jax.numpy as jnp
from jax import lax
from jax.experimental import pallas as pl
from jax.experimental.pallas import tpu as pltpu
from jax.sharding import PartitionSpec as P

ACTIVE = 16
RING = 8
FWD, BWD = 0, 1
OWN, OTHER = 0, 1

norm_eps = 1e-06


def normalize(rows, gain):
    value_rows = rows.astype(jnp.float32)
    scale = lax.rsqrt(jnp.mean(value_rows * value_rows, axis=-1, keepdims=True) + norm_eps)
    return (value_rows * scale * gain).astype(jnp.bfloat16)


def blk_index(x_hi, z, core):
    return x_hi * (2 * RING) + z * 2 + core


def greet(targets):
    barrier = pltpu.get_barrier_semaphore()
    for target in targets:
        pl.semaphore_signal(
            barrier, inc=1, device_id=target, device_id_type=pl.DeviceIdType.MESH
        )
    pl.semaphore_wait(barrier, len(targets))


def remote(src, dst, send_sem, recv_sem, target):
    return pltpu.make_async_remote_copy(
        src_ref=src,
        dst_ref=dst,
        send_sem=send_sem,
        recv_sem=recv_sem,
        device_id=target,
        device_id_type=pl.DeviceIdType.MESH,
    )


def adp_peers(holders):
    me = lax.axis_index("adp")
    return [{"adp": lax.rem(me + step, holders)} for step in range(1, holders)]


def adp_start(holders, own_ref, all_ref, send_sem, recv_sem):
    me = lax.axis_index("adp")
    copies = []
    for step, target in enumerate(adp_peers(holders)):
        copy = remote(own_ref, all_ref.at[me], send_sem.at[step], recv_sem.at[step], target)
        copy.start()
        copies.append(copy)
    return copies


def adp_finish(holders, copies, all_ref, recv_sem, send_sem):
    me = lax.axis_index("adp")
    for step, target in enumerate(adp_peers(holders)):
        source = lax.rem(me + holders - step - 1, holders)
        slab = all_ref.at[source]
        remote(slab, slab, send_sem.at[step], recv_sem.at[step], target).wait_recv()
    for copy in copies:
        copy.wait_send()


def adp_gather_kernel(holders, own_ref, all_ref, send_sem, recv_sem, local_sem):
    me = lax.axis_index("adp")
    greet(adp_peers(holders))
    copies = adp_start(holders, own_ref, all_ref, send_sem, recv_sem)
    keep = pltpu.make_async_copy(own_ref, all_ref.at[me], local_sem)
    keep.start()
    adp_finish(holders, copies, all_ref, recv_sem, send_sem)
    keep.wait()


def adp_gather(own, holders):
    def kernel(*refs):
        adp_gather_kernel(holders, *refs)

    return pl.pallas_call(
        kernel,
        out_shape=jax.ShapeDtypeStruct((holders,) + own.shape, own.dtype),
        in_specs=[pl.BlockSpec(memory_space=pltpu.VMEM)],
        out_specs=pl.BlockSpec(memory_space=pltpu.VMEM),
        scratch_shapes=[
            pltpu.SemaphoreType.DMA((holders - 1,)),
            pltpu.SemaphoreType.DMA((holders - 1,)),
            pltpu.SemaphoreType.DMA,
        ],
        compiler_params=pltpu.CompilerParams(collective_id=1, has_side_effects=True),
        name="adp_gather",
    )(own)


def reach(stream, way):
    return 4 if (stream == OWN) == (way == FWD) else 3


def rows_gather(own, factors, holders):
    blocks = 4 * RING

    def kernel(
        own_ref,
        factor_ref,
        all_ref,
        factor_all_ref,
        ring_send,
        ring_recv,
        across_send,
        across_recv,
        sib_send,
        sib_recv,
        adp_send,
        adp_recv,
        adp_across_send,
        adp_across_recv,
        local_sem,
    ):
        me = lax.axis_index("blk")
        me_adp = lax.axis_index("adp")
        x_hi = me // (2 * RING)
        z = lax.rem(me // 2, RING)
        core = lax.rem(me, 2)
        sibling = {"blk": blk_index(x_hi, z, 1 - core)}
        across = {"blk": blk_index(1 - x_hi, z, core)}
        ahead = {
            FWD: {"blk": blk_index(x_hi, lax.rem(z + 1, RING), core)},
            BWD: {"blk": blk_index(x_hi, lax.rem(z + RING - 1, RING), core)},
        }
        x_lo = lax.rem(me_adp, 2)
        y = me_adp // 2
        adp_across = {"adp": y * 2 + 1 - x_lo}
        adp_ahead = {
            FWD: {"adp": lax.rem(y + 1, RING) * 2 + x_lo},
            BWD: {"adp": lax.rem(y + RING - 1, RING) * 2 + x_lo},
        }
        greet(
            [sibling, across, ahead[FWD], ahead[BWD], adp_across, adp_ahead[FWD], adp_ahead[BWD]]
        )
        sent = []

        def adp_at(stream, way, far):
            x_of = x_lo if stream == OWN else 1 - x_lo
            y_of = lax.rem(y + RING - far, RING) if way == FWD else lax.rem(y + far, RING)
            return y_of * 2 + x_of

        def adp_push(src, index, send_sem, recv_sem, target):
            copy = remote(src, factor_all_ref.at[index], send_sem, recv_sem, target)
            copy.start()
            sent.append(copy)

        def adp_ring(src, index, stream, way, far):
            adp_push(
                src,
                index,
                adp_send.at[stream, way, far],
                adp_recv.at[stream, way, far],
                adp_ahead[way],
            )

        def at(stream, way, far, owner_core):
            x_of = x_hi if stream == OWN else 1 - x_hi
            z_of = lax.rem(z + RING - far, RING) if way == FWD else lax.rem(z + far, RING)
            return blk_index(x_of, z_of, owner_core)

        def push(src, index, send_sem, recv_sem, target):
            copy = remote(src, all_ref.at[index], send_sem, recv_sem, target)
            copy.start()
            sent.append(copy)

        def to_ring(src, index, stream, way, far):
            push(
                src,
                index,
                ring_send.at[stream, way, far],
                ring_recv.at[stream, way, far],
                ahead[way],
            )

        def to_sibling(src, index, stream, way, far):
            push(
                src,
                index,
                sib_send.at[stream, way, far],
                sib_recv.at[stream, way, far],
                sibling,
            )

        push(own_ref, me, across_send, across_recv, across)
        to_ring(own_ref, me, OWN, FWD, 0)
        to_ring(own_ref, me, OWN, BWD, 0)
        to_sibling(own_ref, me, OWN, FWD, 0)
        adp_push(factor_ref, me_adp, adp_across_send, adp_across_recv, adp_across)
        adp_ring(factor_ref, me_adp, OWN, FWD, 0)
        adp_ring(factor_ref, me_adp, OWN, BWD, 0)
        keep = pltpu.make_async_copy(own_ref, all_ref.at[me], local_sem.at[0])
        keep.start()
        keep_factor = pltpu.make_async_copy(factor_ref, factor_all_ref.at[me_adp], local_sem.at[1])
        keep_factor.start()

        other = at(OTHER, FWD, 0, core)
        slab = all_ref.at[other]
        remote(slab, slab, across_send, across_recv, across).wait_recv()
        to_ring(slab, other, OTHER, FWD, 0)
        to_ring(slab, other, OTHER, BWD, 0)
        to_sibling(slab, other, OTHER, FWD, 0)
        adp_other = adp_at(OTHER, FWD, 0)
        slab = factor_all_ref.at[adp_other]
        remote(slab, slab, adp_across_send, adp_across_recv, adp_across).wait_recv()
        adp_ring(slab, adp_other, OTHER, FWD, 0)
        adp_ring(slab, adp_other, OTHER, BWD, 0)
        for far in range(1, 5):
            for stream in (OWN, OTHER):
                for way in (FWD, BWD):
                    last = reach(stream, way)
                    if far > last:
                        continue
                    index = at(stream, way, far, core)
                    slab = all_ref.at[index]
                    remote(
                        slab,
                        slab,
                        ring_send.at[stream, way, far - 1],
                        ring_recv.at[stream, way, far - 1],
                        ahead[way],
                    ).wait_recv()
                    if far < last:
                        to_ring(slab, index, stream, way, far)
                    to_sibling(slab, index, stream, way, far)
                    index = adp_at(stream, way, far)
                    slab = factor_all_ref.at[index]
                    remote(
                        slab,
                        slab,
                        adp_send.at[stream, way, far - 1],
                        adp_recv.at[stream, way, far - 1],
                        adp_ahead[way],
                    ).wait_recv()
                    if far < last:
                        adp_ring(slab, index, stream, way, far)
        for far in range(0, 5):
            for stream in (OWN, OTHER):
                for way in (FWD, BWD):
                    if far > reach(stream, way) or (far == 0 and way == BWD):
                        continue
                    slab = all_ref.at[at(stream, way, far, 1 - core)]
                    remote(
                        slab,
                        slab,
                        sib_send.at[stream, way, far],
                        sib_recv.at[stream, way, far],
                        sibling,
                    ).wait_recv()
        for copy in sent:
            copy.wait_send()
        keep.wait()
        keep_factor.wait()

    dma = pltpu.SemaphoreType.DMA
    return pl.pallas_call(
        kernel,
        out_shape=[
            jax.ShapeDtypeStruct((blocks,) + own.shape, own.dtype),
            jax.ShapeDtypeStruct((holders,) + factors.shape, factors.dtype),
        ],
        in_specs=[pl.BlockSpec(memory_space=pltpu.VMEM)] * 2,
        out_specs=[pl.BlockSpec(memory_space=pltpu.VMEM)] * 2,
        scratch_shapes=[
            dma((2, 2, 4)),
            dma((2, 2, 4)),
            dma,
            dma,
            dma((2, 2, 5)),
            dma((2, 2, 5)),
            dma((2, 2, 4)),
            dma((2, 2, 4)),
            dma,
            dma,
            dma((2,)),
        ],
        compiler_params=pltpu.CompilerParams(collective_id=2, has_side_effects=True),
        name="rows_gather",
    )(own, factors)


def block_scatter(gathered, gate_up, factors, down, stream_rows):
    rows, width = stream_rows.shape
    rank_pairs = gathered.shape[0]
    cat_rows = factors.shape[1]
    kind = gathered.dtype
    piece = width // 6
    minor = (((1,), (1,)), ((), ()))

    def kernel(
        all_ref,
        gate_up_ref,
        factor_ref,
        down_ref,
        stream_ref,
        out_ref,
        group_ref,
        rows_in_ref,
        down_out_ref,
        part_ref,
        sib_ref,
        leave_ref,
        arrive_ref,
        cross_out_ref,
        cross_in_ref,
        ring_send,
        ring_recv,
        across_send,
        across_recv,
        sib_send,
        sib_recv,
    ):
        me = lax.axis_index("blk")
        x_hi = me // (2 * RING)
        z = lax.rem(me // 2, RING)
        core = lax.rem(me, 2)
        sibling = {"blk": blk_index(x_hi, z, 1 - core)}
        across = {"blk": blk_index(1 - x_hi, z, core)}
        ahead = {
            FWD: {"blk": blk_index(x_hi, lax.rem(z + 1, RING), core)},
            BWD: {"blk": blk_index(x_hi, lax.rem(z + RING - 1, RING), core)},
        }
        greet([sibling, across, ahead[FWD], ahead[BWD]])
        sent = []

        def at(stream, way, far, owner_core):
            x_of = x_hi if stream == OWN else 1 - x_hi
            z_of = lax.rem(z + far, RING) if way == FWD else lax.rem(z + RING - far, RING)
            return blk_index(x_of, z_of, owner_core)

        def push(copy):
            copy.start()
            sent.append(copy)

        def keys_at(far):
            return [
                (stream, way, far)
                for stream in (OTHER, OWN)
                for way in (FWD, BWD)
                if far <= reach(stream, way) and not (far == 0 and way == BWD)
            ]

        def sib_copy(stream, way, far):
            return remote(
                part_ref.at[1, stream, way, far],
                sib_ref.at[stream, way, far],
                sib_send.at[stream, way, far],
                sib_recv.at[stream, way, far],
                sibling,
            )

        for k in range(rank_pairs):
            rows_in_ref[k * ACTIVE : (k + 1) * ACTIVE, :] = all_ref[
                k, rows : rows + ACTIVE, :width
            ]
            rank, side = k // 2, k % 2
            for p in range(3):
                start = (side * 3 + p) * piece
                down_out_ref[rank * ACTIVE : (rank + 1) * ACTIVE, start : start + piece] = all_ref[
                    k, p * ACTIVE : (p + 1) * ACTIVE, width : width + piece
                ]

        def compute(far):
            keys = keys_at(far)
            slots = [(side,) + key for side in (1, 0) for key in keys]
            count = len(slots) * rows
            numbers = []
            for place, (side, stream, way, _) in enumerate(slots):
                index = at(stream, way, far, core if side == 0 else 1 - core)
                group_ref[place * rows : (place + 1) * rows, :] = all_ref[index, :rows, :width]
                numbers.append(all_ref[index, :rows, width + piece :].astype(jnp.float32))
            number = jnp.concatenate(numbers, axis=0)
            number = jnp.concatenate([number] * (cat_rows // number.shape[1]), axis=1)
            lane = lax.broadcasted_iota(jnp.int32, (count, cat_rows), 1)
            match = number == lax.rem(lane, ACTIVE).astype(jnp.float32)

            def spread(low):
                return jnp.where(match, low, 0.0).astype(kind)

            group = group_ref[:count, :]
            pre = []
            for side in range(2):
                low = lax.dot_general(
                    group,
                    rows_in_ref[side * cat_rows : (side + 1) * cat_rows, :],
                    minor,
                    preferred_element_type=jnp.float32,
                )
                base = lax.dot_general(
                    group, gate_up_ref[side], minor, preferred_element_type=jnp.float32
                )
                pre.append(
                    base
                    + jnp.dot(spread(low), factor_ref[side], preferred_element_type=jnp.float32)
                )
            hidden = (jax.nn.gelu(pre[0], approximate=True) * pre[1]).astype(kind)
            low = lax.dot_general(
                hidden, factor_ref[2], minor, preferred_element_type=jnp.float32
            )
            part = jnp.dot(hidden, down_ref[...], preferred_element_type=jnp.float32) + jnp.dot(
                spread(low), down_out_ref[...], preferred_element_type=jnp.float32
            )
            part = part.astype(kind)
            for place, slot in enumerate(slots):
                part_ref[slot] = part[place * rows : (place + 1) * rows, :]
            for key in keys:
                push(sib_copy(*key))

        def pair_sum(stream, way, far):
            sib_copy(stream, way, far).wait_recv()
            own = part_ref[0, stream, way, far].astype(jnp.float32)
            return own + sib_ref[stream, way, far].astype(jnp.float32)

        def ring_copy(stream, way, far):
            return remote(
                leave_ref.at[stream, way, far - 1],
                arrive_ref.at[stream, way, far - 1],
                ring_send.at[stream, way, far - 1],
                ring_recv.at[stream, way, far - 1],
                ahead[way],
            )

        def arrived(stream, way, far):
            ring_copy(stream, way, far + 1).wait_recv()
            return arrive_ref[stream, way, far].astype(jnp.float32)

        totals = {}

        def pass_on(far):
            for stream, way, _ in keys_at(far):
                total = pair_sum(stream, way, far)
                if far == 0:
                    total = total + arrived(stream, FWD, 0) + arrived(stream, BWD, 0)
                    if stream == OTHER:
                        cross_out_ref[...] = total.astype(kind)
                        push(remote(cross_out_ref, cross_in_ref, across_send, across_recv, across))
                    else:
                        totals[stream] = total
                    continue
                if far < reach(stream, way):
                    total = total + arrived(stream, way, far)
                leave_ref[stream, way, far - 1] = total.astype(kind)
                push(ring_copy(stream, way, far))

        compute(4)
        for far in range(3, -1, -1):
            compute(far)
            pass_on(far + 1)
        pass_on(0)
        remote(cross_out_ref, cross_in_ref, across_send, across_recv, across).wait_recv()
        total = totals[OWN] + cross_in_ref[...].astype(jnp.float32)
        out_ref[...] = (stream_ref[...].astype(jnp.float32) + total).astype(kind)
        for copy in sent:
            copy.wait_send()

    dma = pltpu.SemaphoreType.DMA
    block = (rows, width)
    return pl.pallas_call(
        kernel,
        out_shape=jax.ShapeDtypeStruct(block, kind),
        in_specs=[pl.BlockSpec(memory_space=pltpu.VMEM)] * 5,
        out_specs=pl.BlockSpec(memory_space=pltpu.VMEM),
        scratch_shapes=[
            pltpu.VMEM((8 * rows, width), kind),
            pltpu.VMEM((2 * cat_rows, width), kind),
            pltpu.VMEM((cat_rows, width), kind),
            pltpu.VMEM((2, 2, 2, 5) + block, kind),
            pltpu.VMEM((2, 2, 5) + block, kind),
            pltpu.VMEM((2, 2, 4) + block, kind),
            pltpu.VMEM((2, 2, 4) + block, kind),
            pltpu.VMEM(block, kind),
            pltpu.VMEM(block, kind),
            dma((2, 2, 4)),
            dma((2, 2, 4)),
            dma,
            dma,
            dma((2, 2, 5)),
            dma((2, 2, 5)),
        ],
        compiler_params=pltpu.CompilerParams(collective_id=3, has_side_effects=True),
        name="block_scatter",
    )(gathered, gate_up, factors, down, stream_rows)


def local(
    stream,
    prenorm_gain,
    gate_up_weight,
    down_weight,
    adapter_gate_input,
    adapter_gate_output,
    adapter_down_input,
    adapter_down_output,
    adapter_of_request,
    request_of_slot,
):
    width = stream.shape[1]
    tok_rows = stream.shape[0]
    hidden_dev = down_weight.shape[0]
    rank_columns = adapter_down_output.shape[1]
    holders = lax.axis_size("adp")
    kept_rows = adapter_gate_input.shape[0]
    catalog = jnp.arange(kept_rows * holders, dtype=jnp.int32)
    used = jnp.any(adapter_of_request[:, None] == catalog[None, :], axis=0)
    order = jnp.cumsum(used.astype(jnp.int32)) - 1
    active_pos = jnp.arange(ACTIVE, dtype=jnp.int32)
    picked = used[None, :] & (order[None, :] == active_pos[:, None])
    active = jnp.sum(jnp.where(picked, catalog[None, :], 0), axis=1)
    table = jnp.arange(adapter_of_request.shape[0], dtype=jnp.int32)
    own_adapter = jnp.sum(
        jnp.where(request_of_slot[:, None] == table[None, :], adapter_of_request[None, :], 0),
        axis=1,
    )
    own_match = own_adapter[:, None] == active[None, :]
    own_slot = jnp.sum(jnp.where(own_match, active_pos[None, :], 0), axis=1)
    normed = normalize(stream, prenorm_gain)
    place = lax.axis_index("blk")
    half = width // 2
    row_in = lax.dynamic_slice_in_dim(adapter_gate_input, place, 1, axis=1)[:, 0]
    row_out = lax.dynamic_slice(
        adapter_down_output, (0, place // 2, lax.rem(place, 2) * half), (kept_rows, 1, half)
    )[:, 0]
    catalog_rows = adp_gather(jnp.concatenate([row_in, row_out], axis=1), holders)
    choose = (active[:, None] == catalog[None, :]).astype(jnp.bfloat16)
    chosen = jnp.dot(
        choose, catalog_rows.reshape(-1, width + half), preferred_element_type=jnp.float32
    ).astype(jnp.bfloat16)
    tile_cols = half // 3
    packed = jnp.concatenate(
        [
            jnp.concatenate([normed, chosen[:, :width]], axis=0),
            jnp.concatenate(
                [chosen[:, width + k * tile_cols : width + (k + 1) * tile_cols] for k in range(3)],
                axis=0,
            ),
            jnp.concatenate(
                [
                    jnp.broadcast_to(own_slot.astype(jnp.bfloat16)[:, None], (tok_rows, 128)),
                    jnp.zeros((ACTIVE, 128), jnp.bfloat16),
                ],
                axis=0,
            ),
        ],
        axis=1,
    )
    own_factors = jnp.concatenate(
        [
            adapter_gate_output.reshape(kept_rows, 2 * rank_columns, hidden_dev),
            adapter_down_input.transpose(0, 2, 1),
        ],
        axis=1,
    )
    gathered, factors = rows_gather(packed, own_factors, holders)
    factors = jnp.take(
        factors.reshape(kept_rows * holders, 3 * rank_columns, hidden_dev), active, axis=0
    ).transpose(1, 0, 2)
    cat_rows = ACTIVE * rank_columns
    factors = factors.reshape(3, cat_rows, hidden_dev)
    return block_scatter(gathered, gate_up_weight, factors, down_weight, stream)


def solution(mesh):
    in_specs = (
        P(("blk", "adp"), None),
        P(),
        P(None, "blk", None),
        P("blk", None),
        P("adp", None, None),
        P("adp", None, None, "blk"),
        P("adp", "blk", None),
        P("adp", None, None),
        P(),
        P(("blk", "adp")),
    )
    out_specs = P(("blk", "adp"), None)
    return jax.shard_map(local, mesh=mesh, in_specs=in_specs, out_specs=out_specs, check_vma=False)
```

```python
import jax
import jax.numpy as jnp
from jax import lax
from jax.experimental import pallas as pl
from jax.experimental.pallas import tpu as pltpu
from jax.sharding import PartitionSpec as P

ACTIVE = 16
RING = 8
FWD, BWD = 0, 1
OWN, OTHER = 0, 1

norm_eps = 1e-06


def normalize(rows, gain):
    value_rows = rows.astype(jnp.float32)
    scale = lax.rsqrt(jnp.mean(value_rows * value_rows, axis=-1, keepdims=True) + norm_eps)
    return (value_rows * scale * gain).astype(jnp.bfloat16)


def blk_index(x_hi, z, core):
    return x_hi * (2 * RING) + z * 2 + core


def greet(targets):
    barrier = pltpu.get_barrier_semaphore()
    for target in targets:
        pl.semaphore_signal(
            barrier, inc=1, device_id=target, device_id_type=pl.DeviceIdType.MESH
        )
    pl.semaphore_wait(barrier, len(targets))


def remote(src, dst, send_sem, recv_sem, target):
    return pltpu.make_async_remote_copy(
        src_ref=src,
        dst_ref=dst,
        send_sem=send_sem,
        recv_sem=recv_sem,
        device_id=target,
        device_id_type=pl.DeviceIdType.MESH,
    )


def reach(stream, way):
    return 4 if (stream == OWN) == (way == FWD) else 3


ROWS, PICKS, FACTORS = 0, 1, 2


def rows_gather(own, catalog_rows, choose, factors, holders):
    blocks = 4 * RING
    kept, catalog_width = catalog_rows.shape
    chunk = catalog_width // 6
    picks = choose.shape[1]

    def kernel(
        own_ref,
        catalog_own_ref,
        choose_ref,
        factor_ref,
        all_ref,
        picks_all_ref,
        factor_all_ref,
        catalog_ref,
        picks_ref,
        ring_send,
        ring_recv,
        across_send,
        across_recv,
        sib_send,
        sib_recv,
        catalog_send,
        catalog_recv,
        local_sem,
    ):
        me = lax.axis_index("blk")
        me_adp = lax.axis_index("adp")
        x_hi = me // (2 * RING)
        z = lax.rem(me // 2, RING)
        core = lax.rem(me, 2)
        x_lo = lax.rem(me_adp, 2)
        y = me_adp // 2
        sibling = {"blk": blk_index(x_hi, z, 1 - core)}
        blk_across = {"blk": blk_index(1 - x_hi, z, core)}
        blk_ahead = {
            FWD: {"blk": blk_index(x_hi, lax.rem(z + 1, RING), core)},
            BWD: {"blk": blk_index(x_hi, lax.rem(z + RING - 1, RING), core)},
        }
        adp_across = {"adp": y * 2 + 1 - x_lo}
        adp_ahead = {
            FWD: {"adp": lax.rem(y + 1, RING) * 2 + x_lo},
            BWD: {"adp": lax.rem(y + RING - 1, RING) * 2 + x_lo},
        }
        adp_peers = [{"adp": lax.rem(me_adp + step, holders)} for step in range(1, holders)]
        across = [blk_across, blk_across, adp_across]
        ahead = [blk_ahead, blk_ahead, adp_ahead]
        source = [own_ref, picks_ref, factor_ref]
        landing = [all_ref, picks_all_ref, factor_all_ref]
        greet([sibling, blk_across, blk_ahead[FWD], blk_ahead[BWD]] + adp_peers)
        sent = []

        def around(at, way, far):
            return lax.rem(at + RING - far, RING) if way == FWD else lax.rem(at + far, RING)

        def index_of(kind, stream, way, far, owner_core):
            if kind == FACTORS:
                return around(y, way, far) * 2 + (x_lo if stream == OWN else 1 - x_lo)
            x_of = x_hi if stream == OWN else 1 - x_hi
            return blk_index(x_of, around(z, way, far), owner_core)

        def push(copy):
            copy.start()
            sent.append(copy)

        def to_ring(src, index, kind, stream, way, far):
            push(
                remote(
                    src,
                    landing[kind].at[index],
                    ring_send.at[kind, stream, way, far],
                    ring_recv.at[kind, stream, way, far],
                    ahead[kind][way],
                )
            )

        def to_sibling(src, index, kind, stream, way, far):
            if kind == FACTORS:
                return
            push(
                remote(
                    src,
                    landing[kind].at[index],
                    sib_send.at[kind, stream, way, far],
                    sib_recv.at[kind, stream, way, far],
                    sibling,
                )
            )

        def launch(kind):
            index = index_of(kind, OWN, FWD, 0, core)
            src = source[kind]
            push(
                remote(
                    src,
                    landing[kind].at[index],
                    across_send.at[kind],
                    across_recv.at[kind],
                    across[kind],
                )
            )
            to_ring(src, index, kind, OWN, FWD, 0)
            to_ring(src, index, kind, OWN, BWD, 0)
            to_sibling(src, index, kind, OWN, FWD, 0)
            keep = pltpu.make_async_copy(src, landing[kind].at[index], local_sem.at[kind])
            keep.start()
            return keep

        def join(kind):
            index = index_of(kind, OTHER, FWD, 0, core)
            slab = landing[kind].at[index]
            remote(
                slab, slab, across_send.at[kind], across_recv.at[kind], across[kind]
            ).wait_recv()
            to_ring(slab, index, kind, OTHER, FWD, 0)
            to_ring(slab, index, kind, OTHER, BWD, 0)
            to_sibling(slab, index, kind, OTHER, FWD, 0)

        def relay(kind, stream, far):
            for way in (FWD, BWD):
                last = reach(stream, way)
                if far > last:
                    continue
                index = index_of(kind, stream, way, far, core)
                slab = landing[kind].at[index]
                remote(
                    slab,
                    slab,
                    ring_send.at[kind, stream, way, far - 1],
                    ring_recv.at[kind, stream, way, far - 1],
                    ahead[kind][way],
                ).wait_recv()
                if far < last:
                    to_ring(slab, index, kind, stream, way, far)
                to_sibling(slab, index, kind, stream, way, far)

        keeps = [launch(ROWS)]
        for step, target in enumerate(adp_peers):
            copy = remote(
                catalog_own_ref,
                catalog_ref.at[me_adp],
                catalog_send.at[step],
                catalog_recv.at[step],
                target,
            )
            push(copy)
        keep = pltpu.make_async_copy(catalog_own_ref, catalog_ref.at[me_adp], local_sem.at[3])
        keep.start()
        keeps.append(launch(FACTORS))
        relay(ROWS, OWN, 1)
        join(ROWS)
        relay(ROWS, OWN, 2)

        for step, target in enumerate(adp_peers):
            slab = catalog_ref.at[lax.rem(me_adp + holders - step - 1, holders)]
            remote(
                slab, slab, catalog_send.at[step], catalog_recv.at[step], target
            ).wait_recv()
        keep.wait()
        for part in range(6):
            cols = slice(part * chunk, (part + 1) * chunk)
            total = jnp.zeros((picks, chunk), jnp.float32)
            for holder in range(holders):
                held = catalog_ref[holder, :, cols].astype(jnp.float32)
                for row in range(kept):
                    mask = jnp.concatenate([choose_ref[holder * kept + row]] * (chunk // 128), axis=1)
                    total = total + mask * held[row : row + 1, :]
            picks_ref[:, cols] = total.astype(picks_ref.dtype)

        keeps.append(launch(PICKS))
        relay(ROWS, OTHER, 1)
        join(FACTORS)
        relay(FACTORS, OWN, 1)
        relay(ROWS, OWN, 3)
        relay(ROWS, OTHER, 2)
        relay(PICKS, OWN, 1)
        join(PICKS)
        relay(FACTORS, OTHER, 1)
        relay(FACTORS, OWN, 2)
        relay(ROWS, OTHER, 3)
        relay(ROWS, OWN, 4)
        relay(PICKS, OWN, 2)
        relay(PICKS, OTHER, 1)
        relay(FACTORS, OTHER, 2)
        relay(FACTORS, OWN, 3)
        relay(ROWS, OTHER, 4)
        relay(PICKS, OWN, 3)
        relay(PICKS, OTHER, 2)
        relay(FACTORS, OTHER, 3)
        relay(FACTORS, OWN, 4)
        relay(PICKS, OTHER, 3)
        relay(PICKS, OWN, 4)
        relay(FACTORS, OTHER, 4)
        relay(PICKS, OTHER, 4)
        for kind in (ROWS, PICKS):
            for far in range(0, 5):
                for stream in (OWN, OTHER):
                    for way in (FWD, BWD):
                        if far > reach(stream, way) or (far == 0 and way == BWD):
                            continue
                        slab = landing[kind].at[index_of(kind, stream, way, far, 1 - core)]
                        remote(
                            slab,
                            slab,
                            sib_send.at[kind, stream, way, far],
                            sib_recv.at[kind, stream, way, far],
                            sibling,
                        ).wait_recv()
        for copy in sent:
            copy.wait_send()
        for keep in keeps:
            keep.wait()

    dma = pltpu.SemaphoreType.DMA
    return pl.pallas_call(
        kernel,
        out_shape=[
            jax.ShapeDtypeStruct((blocks,) + own.shape, own.dtype),
            jax.ShapeDtypeStruct((blocks, picks, catalog_width), own.dtype),
            jax.ShapeDtypeStruct((holders,) + factors.shape, factors.dtype),
        ],
        in_specs=[pl.BlockSpec(memory_space=pltpu.VMEM)] * 4,
        out_specs=[pl.BlockSpec(memory_space=pltpu.VMEM)] * 3,
        scratch_shapes=[
            pltpu.VMEM((holders, kept, catalog_width), own.dtype),
            pltpu.VMEM((picks, catalog_width), own.dtype),
            dma((3, 2, 2, 4)),
            dma((3, 2, 2, 4)),
            dma((3,)),
            dma((3,)),
            dma((2, 2, 2, 5)),
            dma((2, 2, 2, 5)),
            dma((holders - 1,)),
            dma((holders - 1,)),
            dma((4,)),
        ],
        compiler_params=pltpu.CompilerParams(collective_id=2, has_side_effects=True),
        name="rows_gather",
    )(own, catalog_rows, choose, factors)


def block_scatter(gathered, picks, gate_up, factors, down, stream_rows):
    rows, width = stream_rows.shape
    rank_pairs = gathered.shape[0]
    cat_rows = factors.shape[1]
    kind = gathered.dtype
    half = width // 2
    minor = (((1,), (1,)), ((), ()))

    def kernel(
        all_ref,
        picks_ref,
        gate_up_ref,
        factor_ref,
        down_ref,
        stream_ref,
        out_ref,
        group_ref,
        rows_in_ref,
        down_out_ref,
        part_ref,
        sib_ref,
        leave_ref,
        arrive_ref,
        cross_out_ref,
        cross_in_ref,
        ring_send,
        ring_recv,
        across_send,
        across_recv,
        sib_send,
        sib_recv,
    ):
        me = lax.axis_index("blk")
        x_hi = me // (2 * RING)
        z = lax.rem(me // 2, RING)
        core = lax.rem(me, 2)
        sibling = {"blk": blk_index(x_hi, z, 1 - core)}
        across = {"blk": blk_index(1 - x_hi, z, core)}
        ahead = {
            FWD: {"blk": blk_index(x_hi, lax.rem(z + 1, RING), core)},
            BWD: {"blk": blk_index(x_hi, lax.rem(z + RING - 1, RING), core)},
        }
        greet([sibling, across, ahead[FWD], ahead[BWD]])
        sent = []

        def at(stream, way, far, owner_core):
            x_of = x_hi if stream == OWN else 1 - x_hi
            z_of = lax.rem(z + far, RING) if way == FWD else lax.rem(z + RING - far, RING)
            return blk_index(x_of, z_of, owner_core)

        def push(copy):
            copy.start()
            sent.append(copy)

        def keys_at(far):
            return [
                (stream, way, far)
                for stream in (OTHER, OWN)
                for way in (FWD, BWD)
                if far <= reach(stream, way) and not (far == 0 and way == BWD)
            ]

        def sib_copy(stream, way, far):
            return remote(
                part_ref.at[1, stream, way, far],
                sib_ref.at[stream, way, far],
                sib_send.at[stream, way, far],
                sib_recv.at[stream, way, far],
                sibling,
            )

        for k in range(rank_pairs):
            rows_in_ref[k * ACTIVE : (k + 1) * ACTIVE, :] = picks_ref[k, :, :width]
            rank, start = k // 2, (k % 2) * half
            down_out_ref[rank * ACTIVE : (rank + 1) * ACTIVE, start : start + half] = picks_ref[
                k, :, width:
            ]

        def compute(far):
            keys = keys_at(far)
            slots = [(side,) + key for side in (1, 0) for key in keys]
            count = len(slots) * rows
            numbers = []
            for place, (side, stream, way, _) in enumerate(slots):
                index = at(stream, way, far, core if side == 0 else 1 - core)
                group_ref[place * rows : (place + 1) * rows, :] = all_ref[index, :, :width]
                numbers.append(all_ref[index, :, width:].astype(jnp.float32))
            number = jnp.concatenate(numbers, axis=0)
            number = jnp.concatenate([number] * (cat_rows // number.shape[1]), axis=1)
            lane = lax.broadcasted_iota(jnp.int32, (count, cat_rows), 1)
            match = number == lax.rem(lane, ACTIVE).astype(jnp.float32)

            def spread(low):
                return jnp.where(match, low, 0.0).astype(kind)

            group = group_ref[:count, :]
            pre = []
            for side in range(2):
                low = lax.dot_general(
                    group,
                    rows_in_ref[side * cat_rows : (side + 1) * cat_rows, :],
                    minor,
                    preferred_element_type=jnp.float32,
                )
                base = lax.dot_general(
                    group, gate_up_ref[side], minor, preferred_element_type=jnp.float32
                )
                pre.append(
                    base
                    + jnp.dot(spread(low), factor_ref[side], preferred_element_type=jnp.float32)
                )
            hidden = (jax.nn.gelu(pre[0], approximate=True) * pre[1]).astype(kind)
            low = lax.dot_general(
                hidden, factor_ref[2], minor, preferred_element_type=jnp.float32
            )
            part = jnp.dot(hidden, down_ref[...], preferred_element_type=jnp.float32) + jnp.dot(
                spread(low), down_out_ref[...], preferred_element_type=jnp.float32
            )
            part = part.astype(kind)
            for place, slot in enumerate(slots):
                part_ref[slot] = part[place * rows : (place + 1) * rows, :]
            for key in keys:
                push(sib_copy(*key))

        def pair_sum(stream, way, far):
            sib_copy(stream, way, far).wait_recv()
            own = part_ref[0, stream, way, far].astype(jnp.float32)
            return own + sib_ref[stream, way, far].astype(jnp.float32)

        def ring_copy(stream, way, far):
            return remote(
                leave_ref.at[stream, way, far - 1],
                arrive_ref.at[stream, way, far - 1],
                ring_send.at[stream, way, far - 1],
                ring_recv.at[stream, way, far - 1],
                ahead[way],
            )

        def arrived(stream, way, far):
            ring_copy(stream, way, far + 1).wait_recv()
            return arrive_ref[stream, way, far].astype(jnp.float32)

        totals = {}

        def pass_on(far):
            for stream, way, _ in keys_at(far):
                total = pair_sum(stream, way, far)
                if far == 0:
                    total = total + arrived(stream, FWD, 0) + arrived(stream, BWD, 0)
                    if stream == OTHER:
                        cross_out_ref[...] = total.astype(kind)
                        push(remote(cross_out_ref, cross_in_ref, across_send, across_recv, across))
                    else:
                        totals[stream] = total
                    continue
                if far < reach(stream, way):
                    total = total + arrived(stream, way, far)
                leave_ref[stream, way, far - 1] = total.astype(kind)
                push(ring_copy(stream, way, far))

        compute(4)
        for far in range(3, -1, -1):
            compute(far)
            pass_on(far + 1)
        pass_on(0)
        remote(cross_out_ref, cross_in_ref, across_send, across_recv, across).wait_recv()
        total = totals[OWN] + cross_in_ref[...].astype(jnp.float32)
        out_ref[...] = (stream_ref[...].astype(jnp.float32) + total).astype(kind)
        for copy in sent:
            copy.wait_send()

    dma = pltpu.SemaphoreType.DMA
    block = (rows, width)
    return pl.pallas_call(
        kernel,
        out_shape=jax.ShapeDtypeStruct(block, kind),
        in_specs=[pl.BlockSpec(memory_space=pltpu.VMEM)] * 6,
        out_specs=pl.BlockSpec(memory_space=pltpu.VMEM),
        scratch_shapes=[
            pltpu.VMEM((8 * rows, width), kind),
            pltpu.VMEM((2 * cat_rows, width), kind),
            pltpu.VMEM((cat_rows, width), kind),
            pltpu.VMEM((2, 2, 2, 5) + block, kind),
            pltpu.VMEM((2, 2, 5) + block, kind),
            pltpu.VMEM((2, 2, 4) + block, kind),
            pltpu.VMEM((2, 2, 4) + block, kind),
            pltpu.VMEM(block, kind),
            pltpu.VMEM(block, kind),
            dma((2, 2, 4)),
            dma((2, 2, 4)),
            dma,
            dma,
            dma((2, 2, 5)),
            dma((2, 2, 5)),
        ],
        compiler_params=pltpu.CompilerParams(collective_id=3, has_side_effects=True),
        name="block_scatter",
    )(gathered, picks, gate_up, factors, down, stream_rows)


def local(
    stream,
    prenorm_gain,
    gate_up_weight,
    down_weight,
    adapter_gate_input,
    adapter_gate_output,
    adapter_down_input,
    adapter_down_output,
    adapter_of_request,
    request_of_slot,
):
    width = stream.shape[1]
    tok_rows = stream.shape[0]
    hidden_dev = down_weight.shape[0]
    rank_columns = adapter_down_output.shape[1]
    holders = lax.axis_size("adp")
    kept_rows = adapter_gate_input.shape[0]
    catalog = jnp.arange(kept_rows * holders, dtype=jnp.int32)
    used = jnp.any(adapter_of_request[:, None] == catalog[None, :], axis=0)
    order = jnp.cumsum(used.astype(jnp.int32)) - 1
    active_pos = jnp.arange(ACTIVE, dtype=jnp.int32)
    picked = used[None, :] & (order[None, :] == active_pos[:, None])
    active = jnp.sum(jnp.where(picked, catalog[None, :], 0), axis=1)
    table = jnp.arange(adapter_of_request.shape[0], dtype=jnp.int32)
    own_adapter = jnp.sum(
        jnp.where(request_of_slot[:, None] == table[None, :], adapter_of_request[None, :], 0),
        axis=1,
    )
    own_match = own_adapter[:, None] == active[None, :]
    own_slot = jnp.sum(jnp.where(own_match, active_pos[None, :], 0), axis=1)
    normed = normalize(stream, prenorm_gain)
    place = lax.axis_index("blk")
    half = width // 2
    row_in = lax.dynamic_slice_in_dim(adapter_gate_input, place, 1, axis=1)[:, 0]
    row_out = lax.dynamic_slice(
        adapter_down_output, (0, place // 2, lax.rem(place, 2) * half), (kept_rows, 1, half)
    )[:, 0]
    catalog_rows = jnp.concatenate([row_in, row_out], axis=1)
    choose = (catalog[:, None] == active[None, :]).astype(jnp.float32)
    choose = jnp.broadcast_to(choose[:, :, None], choose.shape + (128,))
    packed = jnp.concatenate(
        [normed, jnp.broadcast_to(own_slot.astype(jnp.bfloat16)[:, None], (tok_rows, 128))], axis=1
    )
    own_factors = jnp.concatenate(
        [
            adapter_gate_output.reshape(kept_rows, 2 * rank_columns, hidden_dev),
            adapter_down_input.transpose(0, 2, 1),
        ],
        axis=1,
    )
    gathered, picks, factors = rows_gather(packed, catalog_rows, choose, own_factors, holders)
    factors = jnp.take(
        factors.reshape(kept_rows * holders, 3 * rank_columns, hidden_dev), active, axis=0
    ).transpose(1, 0, 2)
    cat_rows = ACTIVE * rank_columns
    factors = factors.reshape(3, cat_rows, hidden_dev)
    return block_scatter(gathered, picks, gate_up_weight, factors, down_weight, stream)


def solution(mesh):
    in_specs = (
        P(("blk", "adp"), None),
        P(),
        P(None, "blk", None),
        P("blk", None),
        P("adp", None, None),
        P("adp", None, None, "blk"),
        P("adp", "blk", None),
        P("adp", None, None),
        P(),
        P(("blk", "adp")),
    )
    out_specs = P(("blk", "adp"), None)
    return jax.shard_map(local, mesh=mesh, in_specs=in_specs, out_specs=out_specs, check_vma=False)
```

```python
import jax
import jax.numpy as jnp
from jax import lax
from jax.experimental import pallas as pl
from jax.experimental.pallas import tpu as pltpu
from jax.sharding import PartitionSpec as P

ACTIVE = 16
RING = 8
FWD, BWD = 0, 1
OWN, OTHER = 0, 1

norm_eps = 1e-06


def normalize(rows, gain):
    value_rows = rows.astype(jnp.float32)
    scale = lax.rsqrt(jnp.mean(value_rows * value_rows, axis=-1, keepdims=True) + norm_eps)
    return (value_rows * scale * gain).astype(jnp.bfloat16)


def blk_index(x_hi, z, core):
    return x_hi * (2 * RING) + z * 2 + core


def greet(targets):
    barrier = pltpu.get_barrier_semaphore()
    for target in targets:
        pl.semaphore_signal(
            barrier, inc=1, device_id=target, device_id_type=pl.DeviceIdType.MESH
        )
    pl.semaphore_wait(barrier, len(targets))


def remote(src, dst, send_sem, recv_sem, target):
    return pltpu.make_async_remote_copy(
        src_ref=src,
        dst_ref=dst,
        send_sem=send_sem,
        recv_sem=recv_sem,
        device_id=target,
        device_id_type=pl.DeviceIdType.MESH,
    )


def reach(stream, way):
    return 4 if (stream == OWN) == (way == FWD) else 3


ROWS, PICKS, FACTORS = 0, 1, 2


def sublayer(own, catalog_rows, choose, factors, active, gate_up, down, stream_rows, holders):
    blocks = 4 * RING
    kept, catalog_width = catalog_rows.shape
    chunk = catalog_width // 6
    picks = choose.shape[1]
    rows, width = stream_rows.shape
    factor_rows, hidden_dev = factors.shape[1:]
    cat_rows = picks * factor_rows // 3
    rank_pairs = blocks
    kind = own.dtype
    half = width // 2
    minor = (((1,), (1,)), ((), ()))

    def kernel(
        own_ref,
        catalog_own_ref,
        choose_ref,
        factor_ref,
        active_ref,
        gate_up_ref,
        down_ref,
        stream_ref,
        out_ref,
        all_ref,
        picks_all_ref,
        factor_all_ref,
        catalog_ref,
        picks_ref,
        wide_low_ref,
        wide_high_ref,
        active_factor_ref,
        group_ref,
        rows_in_ref,
        down_out_ref,
        part_ref,
        sib_ref,
        leave_ref,
        arrive_ref,
        cross_out_ref,
        cross_in_ref,
        ring_send,
        ring_recv,
        across_send,
        across_recv,
        sib_send,
        sib_recv,
        catalog_send,
        catalog_recv,
        local_sem,
        sum_ring_send,
        sum_ring_recv,
        sum_across_send,
        sum_across_recv,
        sum_sib_send,
        sum_sib_recv,
    ):
        me = lax.axis_index("blk")
        me_adp = lax.axis_index("adp")
        x_hi = me // (2 * RING)
        z = lax.rem(me // 2, RING)
        core = lax.rem(me, 2)
        x_lo = lax.rem(me_adp, 2)
        y = me_adp // 2
        sibling = {"blk": blk_index(x_hi, z, 1 - core)}
        blk_across = {"blk": blk_index(1 - x_hi, z, core)}
        blk_ahead = {
            FWD: {"blk": blk_index(x_hi, lax.rem(z + 1, RING), core)},
            BWD: {"blk": blk_index(x_hi, lax.rem(z + RING - 1, RING), core)},
        }
        adp_across = {"adp": y * 2 + 1 - x_lo}
        adp_ahead = {
            FWD: {"adp": lax.rem(y + 1, RING) * 2 + x_lo},
            BWD: {"adp": lax.rem(y + RING - 1, RING) * 2 + x_lo},
        }
        adp_peers = [{"adp": lax.rem(me_adp + step, holders)} for step in range(1, holders)]
        across = [blk_across, blk_across, adp_across]
        ahead = [blk_ahead, blk_ahead, adp_ahead]
        source = [own_ref, picks_ref, factor_ref]
        landing = [all_ref, picks_all_ref, factor_all_ref]
        greet([sibling, blk_across, blk_ahead[FWD], blk_ahead[BWD]] + adp_peers)
        sent = []

        def around(at, way, far):
            return lax.rem(at + RING - far, RING) if way == FWD else lax.rem(at + far, RING)

        def index_of(kind, stream, way, far, owner_core):
            if kind == FACTORS:
                return around(y, way, far) * 2 + (x_lo if stream == OWN else 1 - x_lo)
            x_of = x_hi if stream == OWN else 1 - x_hi
            return blk_index(x_of, around(z, way, far), owner_core)

        def push(copy):
            copy.start()
            sent.append(copy)

        def to_ring(src, index, kind, stream, way, far):
            push(
                remote(
                    src,
                    landing[kind].at[index],
                    ring_send.at[kind, stream, way, far],
                    ring_recv.at[kind, stream, way, far],
                    ahead[kind][way],
                )
            )

        def to_sibling(src, index, kind, stream, way, far):
            if kind == FACTORS:
                return
            push(
                remote(
                    src,
                    landing[kind].at[index],
                    sib_send.at[kind, stream, way, far],
                    sib_recv.at[kind, stream, way, far],
                    sibling,
                )
            )

        def launch(kind):
            index = index_of(kind, OWN, FWD, 0, core)
            src = source[kind]
            push(
                remote(
                    src,
                    landing[kind].at[index],
                    across_send.at[kind],
                    across_recv.at[kind],
                    across[kind],
                )
            )
            to_ring(src, index, kind, OWN, FWD, 0)
            to_ring(src, index, kind, OWN, BWD, 0)
            to_sibling(src, index, kind, OWN, FWD, 0)
            keep = pltpu.make_async_copy(src, landing[kind].at[index], local_sem.at[kind])
            keep.start()
            return keep

        def join(kind):
            index = index_of(kind, OTHER, FWD, 0, core)
            slab = landing[kind].at[index]
            remote(
                slab, slab, across_send.at[kind], across_recv.at[kind], across[kind]
            ).wait_recv()
            to_ring(slab, index, kind, OTHER, FWD, 0)
            to_ring(slab, index, kind, OTHER, BWD, 0)
            to_sibling(slab, index, kind, OTHER, FWD, 0)

        def relay(kind, stream, far):
            for way in (FWD, BWD):
                last = reach(stream, way)
                if far > last:
                    continue
                index = index_of(kind, stream, way, far, core)
                slab = landing[kind].at[index]
                remote(
                    slab,
                    slab,
                    ring_send.at[kind, stream, way, far - 1],
                    ring_recv.at[kind, stream, way, far - 1],
                    ahead[kind][way],
                ).wait_recv()
                if far < last:
                    to_ring(slab, index, kind, stream, way, far)
                to_sibling(slab, index, kind, stream, way, far)

        keeps = [launch(ROWS)]
        for step, target in enumerate(adp_peers):
            copy = remote(
                catalog_own_ref,
                catalog_ref.at[me_adp],
                catalog_send.at[step],
                catalog_recv.at[step],
                target,
            )
            push(copy)
        keep = pltpu.make_async_copy(catalog_own_ref, catalog_ref.at[me_adp], local_sem.at[3])
        keep.start()
        relay(ROWS, OWN, 1)
        join(ROWS)
        relay(ROWS, OWN, 2)

        for step, target in enumerate(adp_peers):
            slab = catalog_ref.at[lax.rem(me_adp + holders - step - 1, holders)]
            remote(
                slab, slab, catalog_send.at[step], catalog_recv.at[step], target
            ).wait_recv()
        keep.wait()
        keeps.append(launch(FACTORS))
        for part in range(6):
            cols = slice(part * chunk, (part + 1) * chunk)
            total = jnp.zeros((picks, chunk), jnp.float32)
            for holder in range(holders):
                held = catalog_ref[holder, :, cols].astype(jnp.float32)
                for row in range(kept):
                    mask = jnp.concatenate([choose_ref[holder * kept + row]] * (chunk // 128), axis=1)
                    total = total + mask * held[row : row + 1, :]
            picks_ref[:, cols] = total.astype(picks_ref.dtype)

        keeps.append(launch(PICKS))
        relay(ROWS, OTHER, 1)
        join(FACTORS)
        relay(FACTORS, OWN, 1)
        relay(ROWS, OWN, 3)
        relay(ROWS, OTHER, 2)
        relay(PICKS, OWN, 1)
        join(PICKS)
        relay(FACTORS, OTHER, 1)
        relay(FACTORS, OWN, 2)
        relay(ROWS, OTHER, 3)
        relay(ROWS, OWN, 4)
        relay(PICKS, OWN, 2)
        relay(PICKS, OTHER, 1)
        relay(FACTORS, OTHER, 2)
        relay(FACTORS, OWN, 3)
        relay(ROWS, OTHER, 4)
        relay(PICKS, OWN, 3)
        relay(PICKS, OTHER, 2)
        relay(FACTORS, OTHER, 3)
        relay(FACTORS, OWN, 4)
        relay(PICKS, OTHER, 3)
        relay(PICKS, OWN, 4)
        relay(FACTORS, OTHER, 4)
        relay(PICKS, OTHER, 4)
        for keep in keeps:
            keep.wait()
        for place in range(picks):
            number = active_ref[place]
            slab = factor_all_ref[number // kept, lax.rem(number, kept)].astype(jnp.float32)
            spare = jnp.zeros((factor_rows, 256 - hidden_dev), jnp.float32)
            slab = jnp.concatenate([slab, spare], axis=1)
            spots = pl.ds(place, factor_rows, stride=picks)
            wide_low_ref[spots, :] = slab[:, :128]
            wide_high_ref[spots, :] = slab[:, 128:]
        wide = jnp.concatenate([wide_low_ref[...], wide_high_ref[...]], axis=1)[:, :hidden_dev]
        active_factor_ref[...] = wide.astype(kind).reshape(active_factor_ref.shape)
        for slabs in (ROWS, PICKS):
            for far in range(0, 5):
                for stream in (OWN, OTHER):
                    for way in (FWD, BWD):
                        if far > reach(stream, way) or (far == 0 and way == BWD):
                            continue
                        slab = landing[slabs].at[index_of(slabs, stream, way, far, 1 - core)]
                        remote(
                            slab,
                            slab,
                            sib_send.at[slabs, stream, way, far],
                            sib_recv.at[slabs, stream, way, far],
                            sibling,
                        ).wait_recv()

        def at(stream, way, far, owner_core):
            x_of = x_hi if stream == OWN else 1 - x_hi
            z_of = lax.rem(z + far, RING) if way == FWD else lax.rem(z + RING - far, RING)
            return blk_index(x_of, z_of, owner_core)

        def keys_at(far):
            return [
                (stream, way, far)
                for stream in (OTHER, OWN)
                for way in (FWD, BWD)
                if far <= reach(stream, way) and not (far == 0 and way == BWD)
            ]

        def sib_copy(stream, way, far):
            return remote(
                part_ref.at[1, stream, way, far],
                sib_ref.at[stream, way, far],
                sum_sib_send.at[stream, way, far],
                sum_sib_recv.at[stream, way, far],
                sibling,
            )

        for k in range(rank_pairs):
            rows_in_ref[k * ACTIVE : (k + 1) * ACTIVE, :] = picks_all_ref[k, :, :width]
            rank, start = k // 2, (k % 2) * half
            down_out_ref[rank * ACTIVE : (rank + 1) * ACTIVE, start : start + half] = picks_all_ref[
                k, :, width:
            ]

        def compute(far):
            keys = keys_at(far)
            slots = [(side,) + key for side in (1, 0) for key in keys]
            count = len(slots) * rows
            numbers = []
            for place, (side, stream, way, _) in enumerate(slots):
                index = at(stream, way, far, core if side == 0 else 1 - core)
                group_ref[place * rows : (place + 1) * rows, :] = all_ref[index, :, :width]
                numbers.append(all_ref[index, :, width:].astype(jnp.float32))
            number = jnp.concatenate(numbers, axis=0)
            number = jnp.concatenate([number] * (cat_rows // number.shape[1]), axis=1)
            lane = lax.broadcasted_iota(jnp.int32, (count, cat_rows), 1)
            match = number == lax.rem(lane, ACTIVE).astype(jnp.float32)

            def spread(low):
                return jnp.where(match, low, 0.0).astype(kind)

            group = group_ref[:count, :]
            pre = []
            for side in range(2):
                low = lax.dot_general(
                    group,
                    rows_in_ref[side * cat_rows : (side + 1) * cat_rows, :],
                    minor,
                    preferred_element_type=jnp.float32,
                )
                base = lax.dot_general(
                    group, gate_up_ref[side], minor, preferred_element_type=jnp.float32
                )
                pre.append(
                    base
                    + jnp.dot(spread(low), active_factor_ref[side], preferred_element_type=jnp.float32)
                )
            hidden = (jax.nn.gelu(pre[0], approximate=True) * pre[1]).astype(kind)
            low = lax.dot_general(
                hidden, active_factor_ref[2], minor, preferred_element_type=jnp.float32
            )
            part = jnp.dot(hidden, down_ref[...], preferred_element_type=jnp.float32) + jnp.dot(
                spread(low), down_out_ref[...], preferred_element_type=jnp.float32
            )
            part = part.astype(kind)
            for place, slot in enumerate(slots):
                part_ref[slot] = part[place * rows : (place + 1) * rows, :]
            for key in keys:
                push(sib_copy(*key))

        def pair_sum(stream, way, far):
            sib_copy(stream, way, far).wait_recv()
            own = part_ref[0, stream, way, far].astype(jnp.float32)
            return own + sib_ref[stream, way, far].astype(jnp.float32)

        def ring_copy(stream, way, far):
            return remote(
                leave_ref.at[stream, way, far - 1],
                arrive_ref.at[stream, way, far - 1],
                sum_ring_send.at[stream, way, far - 1],
                sum_ring_recv.at[stream, way, far - 1],
                blk_ahead[way],
            )

        def arrived(stream, way, far):
            ring_copy(stream, way, far + 1).wait_recv()
            return arrive_ref[stream, way, far].astype(jnp.float32)

        totals = {}

        def pass_on(far):
            for stream, way, _ in keys_at(far):
                total = pair_sum(stream, way, far)
                if far == 0:
                    total = total + arrived(stream, FWD, 0) + arrived(stream, BWD, 0)
                    if stream == OTHER:
                        cross_out_ref[...] = total.astype(kind)
                        push(remote(cross_out_ref, cross_in_ref, sum_across_send, sum_across_recv, blk_across))
                    else:
                        totals[stream] = total
                    continue
                if far < reach(stream, way):
                    total = total + arrived(stream, way, far)
                leave_ref[stream, way, far - 1] = total.astype(kind)
                push(ring_copy(stream, way, far))

        compute(4)
        for far in range(3, -1, -1):
            compute(far)
            pass_on(far + 1)
        pass_on(0)
        remote(cross_out_ref, cross_in_ref, sum_across_send, sum_across_recv, blk_across).wait_recv()
        total = totals[OWN] + cross_in_ref[...].astype(jnp.float32)
        out_ref[...] = (stream_ref[...].astype(jnp.float32) + total).astype(kind)
        for copy in sent:
            copy.wait_send()

    dma = pltpu.SemaphoreType.DMA
    block = (rows, width)
    vmem = pl.BlockSpec(memory_space=pltpu.VMEM)
    return pl.pallas_call(
        kernel,
        out_shape=jax.ShapeDtypeStruct(block, kind),
        in_specs=[vmem] * 4 + [pl.BlockSpec(memory_space=pltpu.SMEM)] + [vmem] * 3,
        out_specs=vmem,
        scratch_shapes=[
            pltpu.VMEM((blocks,) + own.shape, kind),
            pltpu.VMEM((blocks, picks, catalog_width), kind),
            pltpu.VMEM((holders,) + factors.shape, kind),
            pltpu.VMEM((holders, kept, catalog_width), kind),
            pltpu.VMEM((picks, catalog_width), kind),
            pltpu.VMEM((picks * factor_rows, 128), jnp.float32),
            pltpu.VMEM((picks * factor_rows, 128), jnp.float32),
            pltpu.VMEM((3, cat_rows, hidden_dev), kind),
            pltpu.VMEM((8 * rows, width), kind),
            pltpu.VMEM((2 * cat_rows, width), kind),
            pltpu.VMEM((cat_rows, width), kind),
            pltpu.VMEM((2, 2, 2, 5) + block, kind),
            pltpu.VMEM((2, 2, 5) + block, kind),
            pltpu.VMEM((2, 2, 4) + block, kind),
            pltpu.VMEM((2, 2, 4) + block, kind),
            pltpu.VMEM(block, kind),
            pltpu.VMEM(block, kind),
            dma((3, 2, 2, 4)),
            dma((3, 2, 2, 4)),
            dma((3,)),
            dma((3,)),
            dma((2, 2, 2, 5)),
            dma((2, 2, 2, 5)),
            dma((holders - 1,)),
            dma((holders - 1,)),
            dma((4,)),
            dma((2, 2, 4)),
            dma((2, 2, 4)),
            dma,
            dma,
            dma((2, 2, 5)),
            dma((2, 2, 5)),
        ],
        compiler_params=pltpu.CompilerParams(collective_id=1, has_side_effects=True),
        name="sublayer",
    )(own, catalog_rows, choose, factors, active, gate_up, down, stream_rows)


def local(
    stream,
    prenorm_gain,
    gate_up_weight,
    down_weight,
    adapter_gate_input,
    adapter_gate_output,
    adapter_down_input,
    adapter_down_output,
    adapter_of_request,
    request_of_slot,
):
    width = stream.shape[1]
    tok_rows = stream.shape[0]
    hidden_dev = down_weight.shape[0]
    rank_columns = adapter_down_output.shape[1]
    holders = lax.axis_size("adp")
    kept_rows = adapter_gate_input.shape[0]
    catalog = jnp.arange(kept_rows * holders, dtype=jnp.int32)
    used = jnp.any(adapter_of_request[:, None] == catalog[None, :], axis=0)
    order = jnp.cumsum(used.astype(jnp.int32)) - 1
    active_pos = jnp.arange(ACTIVE, dtype=jnp.int32)
    picked = used[None, :] & (order[None, :] == active_pos[:, None])
    active = jnp.sum(jnp.where(picked, catalog[None, :], 0), axis=1)
    table = jnp.arange(adapter_of_request.shape[0], dtype=jnp.int32)
    own_adapter = jnp.sum(
        jnp.where(request_of_slot[:, None] == table[None, :], adapter_of_request[None, :], 0),
        axis=1,
    )
    own_match = own_adapter[:, None] == active[None, :]
    own_slot = jnp.sum(jnp.where(own_match, active_pos[None, :], 0), axis=1)
    normed = normalize(stream, prenorm_gain)
    place = lax.axis_index("blk")
    half = width // 2
    row_in = lax.dynamic_slice_in_dim(adapter_gate_input, place, 1, axis=1)[:, 0]
    row_out = lax.dynamic_slice(
        adapter_down_output, (0, place // 2, lax.rem(place, 2) * half), (kept_rows, 1, half)
    )[:, 0]
    catalog_rows = jnp.concatenate([row_in, row_out], axis=1)
    choose = (catalog[:, None] == active[None, :]).astype(jnp.float32)
    choose = jnp.broadcast_to(choose[:, :, None], choose.shape + (128,))
    packed = jnp.concatenate(
        [normed, jnp.broadcast_to(own_slot.astype(jnp.bfloat16)[:, None], (tok_rows, 128))], axis=1
    )
    own_factors = jnp.concatenate(
        [
            adapter_gate_output.reshape(kept_rows, 2 * rank_columns, hidden_dev),
            adapter_down_input.transpose(0, 2, 1),
        ],
        axis=1,
    )
    return sublayer(
        packed,
        catalog_rows,
        choose,
        own_factors,
        active,
        gate_up_weight,
        down_weight,
        stream,
        holders,
    )


def solution(mesh):
    in_specs = (
        P(("blk", "adp"), None),
        P(),
        P(None, "blk", None),
        P("blk", None),
        P("adp", None, None),
        P("adp", None, None, "blk"),
        P("adp", "blk", None),
        P("adp", None, None),
        P(),
        P(("blk", "adp")),
    )
    out_specs = P(("blk", "adp"), None)
    return jax.shard_map(local, mesh=mesh, in_specs=in_specs, out_specs=out_specs, check_vma=False)
```

```python
import jax
import jax.numpy as jnp
from jax import lax
from jax.experimental import pallas as pl
from jax.experimental.pallas import tpu as pltpu
from jax.sharding import PartitionSpec as P

ACTIVE = 16
RING = 8
FWD, BWD = 0, 1
OWN, OTHER = 0, 1

norm_eps = 1e-06


def normalize(rows, gain):
    value_rows = rows.astype(jnp.float32)
    scale = lax.rsqrt(jnp.mean(value_rows * value_rows, axis=-1, keepdims=True) + norm_eps)
    return (value_rows * scale * gain).astype(jnp.bfloat16)


def blk_index(x_hi, z, core):
    return x_hi * (2 * RING) + z * 2 + core


def greet(targets):
    barrier = pltpu.get_barrier_semaphore()
    for target in targets:
        pl.semaphore_signal(
            barrier, inc=1, device_id=target, device_id_type=pl.DeviceIdType.MESH
        )


def remote(src, dst, send_sem, recv_sem, target):
    return pltpu.make_async_remote_copy(
        src_ref=src,
        dst_ref=dst,
        send_sem=send_sem,
        recv_sem=recv_sem,
        device_id=target,
        device_id_type=pl.DeviceIdType.MESH,
    )


def reach(stream, way):
    return 4 if (stream == OWN) == (way == FWD) else 3


ROWS, PICKS, FACTORS = 0, 1, 2


def sublayer(
    stream_rows,
    gain,
    slots,
    gate_in,
    down_out,
    active_rows,
    factors,
    active,
    gate_up,
    down,
    holders,
):
    blocks = 4 * RING
    kept = gate_in.shape[0]
    rows, width = stream_rows.shape
    packed_width = width + slots.shape[1]
    catalog_width = width + width // 2
    chunk = catalog_width // 6
    picks = active_rows.shape[0]
    factor_rows, hidden_dev = factors.shape[1:]
    cat_rows = picks * factor_rows // 3
    rank_pairs = blocks
    kind = stream_rows.dtype
    half = width // 2
    minor = (((1,), (1,)), ((), ()))

    def kernel(
        stream_ref,
        gain_ref,
        slots_ref,
        gate_in_ref,
        down_out_ref,
        active_rows_ref,
        factor_ref,
        active_ref,
        gate_up_ref,
        down_ref,
        out_ref,
        own_ref,
        catalog_own_ref,
        all_ref,
        picks_all_ref,
        factor_all_ref,
        catalog_ref,
        picks_ref,
        wide_low_ref,
        wide_high_ref,
        active_factor_ref,
        group_ref,
        part_ref,
        sib_ref,
        leave_ref,
        arrive_ref,
        cross_out_ref,
        cross_in_ref,
        ring_send,
        ring_recv,
        across_send,
        across_recv,
        sib_send,
        sib_recv,
        catalog_send,
        catalog_recv,
        local_sem,
        sum_ring_send,
        sum_ring_recv,
        sum_across_send,
        sum_across_recv,
        sum_sib_send,
        sum_sib_recv,
    ):
        me = lax.axis_index("blk")
        me_adp = lax.axis_index("adp")
        x_hi = me // (2 * RING)
        z = lax.rem(me // 2, RING)
        core = lax.rem(me, 2)
        x_lo = lax.rem(me_adp, 2)
        y = me_adp // 2
        sibling = {"blk": blk_index(x_hi, z, 1 - core)}
        blk_across = {"blk": blk_index(1 - x_hi, z, core)}
        blk_ahead = {
            FWD: {"blk": blk_index(x_hi, lax.rem(z + 1, RING), core)},
            BWD: {"blk": blk_index(x_hi, lax.rem(z + RING - 1, RING), core)},
        }
        adp_across = {"adp": y * 2 + 1 - x_lo}
        adp_ahead = {
            FWD: {"adp": lax.rem(y + 1, RING) * 2 + x_lo},
            BWD: {"adp": lax.rem(y + RING - 1, RING) * 2 + x_lo},
        }
        adp_peers = [{"adp": lax.rem(me_adp + step, holders)} for step in range(1, holders)]
        across = [blk_across, blk_across, adp_across]
        ahead = [blk_ahead, blk_ahead, adp_ahead]
        source = [own_ref, picks_ref, factor_ref]
        landing = [all_ref, picks_all_ref, factor_all_ref]
        greeted = [sibling, blk_across, blk_ahead[FWD], blk_ahead[BWD]] + adp_peers
        greet(greeted)

        def pick_row(table, at_row):
            place = lax.broadcasted_iota(jnp.int32, table.shape, 0)
            kept_row = jnp.where(place == at_row, table.astype(jnp.float32), 0.0)
            return jnp.sum(kept_row, axis=0, keepdims=True)

        out_rows = [pick_row(down_out_ref[row], me // 2) for row in range(kept)]
        in_rows = [pick_row(gate_in_ref[row], me) for row in range(kept)]
        in_rows = jnp.concatenate(in_rows, axis=0)
        out_rows = jnp.concatenate(out_rows, axis=0)
        catalog_own_ref[:, :width] = in_rows.astype(kind)
        catalog_own_ref[:, width:] = jnp.where(
            core == 0, out_rows[:, :half], out_rows[:, half:]
        ).astype(kind)
        own_ref[:, :width] = normalize(stream_ref[...], gain_ref[...])
        own_ref[:, width:] = slots_ref[...]
        pl.semaphore_wait(pltpu.get_barrier_semaphore(), len(greeted))
        sent = []

        def around(at, way, far):
            return lax.rem(at + RING - far, RING) if way == FWD else lax.rem(at + far, RING)

        def index_of(kind, stream, way, far, owner_core):
            if kind == FACTORS:
                return around(y, way, far) * 2 + (x_lo if stream == OWN else 1 - x_lo)
            x_of = x_hi if stream == OWN else 1 - x_hi
            return blk_index(x_of, around(z, way, far), owner_core)

        def push(copy):
            copy.start()
            sent.append(copy)

        def to_ring(src, index, kind, stream, way, far):
            push(
                remote(
                    src,
                    landing[kind].at[index],
                    ring_send.at[kind, stream, way, far],
                    ring_recv.at[kind, stream, way, far],
                    ahead[kind][way],
                )
            )

        def to_sibling(src, index, kind, stream, way, far):
            if kind == FACTORS:
                return
            push(
                remote(
                    src,
                    landing[kind].at[index],
                    sib_send.at[kind, stream, way, far],
                    sib_recv.at[kind, stream, way, far],
                    sibling,
                )
            )

        def launch(kind):
            index = index_of(kind, OWN, FWD, 0, core)
            src = source[kind]
            push(
                remote(
                    src,
                    landing[kind].at[index],
                    across_send.at[kind],
                    across_recv.at[kind],
                    across[kind],
                )
            )
            to_ring(src, index, kind, OWN, FWD, 0)
            to_ring(src, index, kind, OWN, BWD, 0)
            to_sibling(src, index, kind, OWN, FWD, 0)
            keep = pltpu.make_async_copy(src, landing[kind].at[index], local_sem.at[kind])
            keep.start()
            return keep

        def join(kind):
            index = index_of(kind, OTHER, FWD, 0, core)
            slab = landing[kind].at[index]
            remote(
                slab, slab, across_send.at[kind], across_recv.at[kind], across[kind]
            ).wait_recv()
            to_ring(slab, index, kind, OTHER, FWD, 0)
            to_ring(slab, index, kind, OTHER, BWD, 0)
            to_sibling(slab, index, kind, OTHER, FWD, 0)

        def relay(kind, stream, far):
            for way in (FWD, BWD):
                last = reach(stream, way)
                if far > last:
                    continue
                index = index_of(kind, stream, way, far, core)
                slab = landing[kind].at[index]
                remote(
                    slab,
                    slab,
                    ring_send.at[kind, stream, way, far - 1],
                    ring_recv.at[kind, stream, way, far - 1],
                    ahead[kind][way],
                ).wait_recv()
                if far < last:
                    to_ring(slab, index, kind, stream, way, far)
                to_sibling(slab, index, kind, stream, way, far)

        keeps = []
        for step, target in enumerate(adp_peers):
            copy = remote(
                catalog_own_ref,
                catalog_ref.at[me_adp],
                catalog_send.at[step],
                catalog_recv.at[step],
                target,
            )
            push(copy)
        keeps.append(launch(ROWS))
        keep = pltpu.make_async_copy(catalog_own_ref, catalog_ref.at[me_adp], local_sem.at[3])
        keep.start()
        relay(ROWS, OWN, 1)
        join(ROWS)
        relay(ROWS, OWN, 2)

        for step, target in enumerate(adp_peers):
            slab = catalog_ref.at[lax.rem(me_adp + holders - step - 1, holders)]
            remote(
                slab, slab, catalog_send.at[step], catalog_recv.at[step], target
            ).wait_recv()
        keep.wait()
        keeps.append(launch(FACTORS))
        for part in range(6):
            cols = slice(part * chunk, (part + 1) * chunk)
            total = jnp.zeros((picks, chunk), jnp.float32)
            for holder in range(holders):
                held = catalog_ref[holder, :, cols].astype(jnp.float32)
                for row in range(kept):
                    number = float(holder * kept + row)
                    mask = jnp.where(active_rows_ref[...] == number, 1.0, 0.0)
                    mask = jnp.concatenate([mask] * (chunk // 128), axis=1)
                    total = total + mask * held[row : row + 1, :]
            picks_ref[:, cols] = total.astype(picks_ref.dtype)

        keeps.append(launch(PICKS))
        relay(ROWS, OTHER, 1)
        join(FACTORS)
        relay(FACTORS, OWN, 1)
        relay(ROWS, OWN, 3)
        relay(ROWS, OTHER, 2)
        relay(PICKS, OWN, 1)
        join(PICKS)
        relay(FACTORS, OTHER, 1)
        relay(FACTORS, OWN, 2)
        relay(ROWS, OTHER, 3)
        relay(ROWS, OWN, 4)
        relay(PICKS, OWN, 2)
        relay(PICKS, OTHER, 1)
        relay(FACTORS, OTHER, 2)
        relay(FACTORS, OWN, 3)
        relay(ROWS, OTHER, 4)
        relay(PICKS, OWN, 3)
        relay(PICKS, OTHER, 2)
        relay(FACTORS, OTHER, 3)
        relay(FACTORS, OWN, 4)
        relay(PICKS, OTHER, 3)
        relay(PICKS, OWN, 4)
        relay(FACTORS, OTHER, 4)
        def at(stream, way, far, owner_core):
            x_of = x_hi if stream == OWN else 1 - x_hi
            z_of = lax.rem(z + far, RING) if way == FWD else lax.rem(z + RING - far, RING)
            return blk_index(x_of, z_of, owner_core)

        def settle(slabs):
            for far in range(0, 5):
                for stream in (OWN, OTHER):
                    for way in (FWD, BWD):
                        if far > reach(stream, way) or (far == 0 and way == BWD):
                            continue
                        slab = landing[slabs].at[index_of(slabs, stream, way, far, 1 - core)]
                        remote(
                            slab,
                            slab,
                            sib_send.at[slabs, stream, way, far],
                            sib_recv.at[slabs, stream, way, far],
                            sibling,
                        ).wait_recv()

        def keys_at(far):
            return [
                (stream, way, far)
                for stream in (OTHER, OWN)
                for way in (FWD, BWD)
                if far <= reach(stream, way) and not (far == 0 and way == BWD)
            ]

        def sib_copy(stream, way, far):
            return remote(
                part_ref.at[1, stream, way, far],
                sib_ref.at[stream, way, far],
                sum_sib_send.at[stream, way, far],
                sum_sib_recv.at[stream, way, far],
                sibling,
            )

        def slots_at(far):
            return [(side,) + key for side in (1, 0) for key in keys_at(far)]

        def base_of(far):
            slots = slots_at(far)
            for place, (side, stream, way, _) in enumerate(slots):
                index = at(stream, way, far, core if side == 0 else 1 - core)
                group_ref[place * rows : (place + 1) * rows, :] = all_ref[index, :, :width]
            group = group_ref[: len(slots) * rows, :]
            return [
                lax.dot_general(
                    group, gate_up_ref[side], minor, preferred_element_type=jnp.float32
                )
                for side in range(2)
            ]

        def compute(far, base):
            keys = keys_at(far)
            slots = slots_at(far)
            count = len(slots) * rows
            numbers = []
            for place, (side, stream, way, _) in enumerate(slots):
                index = at(stream, way, far, core if side == 0 else 1 - core)
                numbers.append(all_ref[index, :, width:].astype(jnp.float32))
            number = jnp.concatenate(numbers, axis=0)
            number = jnp.concatenate([number] * (cat_rows // number.shape[1]), axis=1)
            lane = lax.broadcasted_iota(jnp.int32, (count, cat_rows), 1)
            match = number == lax.rem(lane, ACTIVE).astype(jnp.float32)

            def spread(low):
                return jnp.where(match, low, 0.0).astype(kind)

            group = group_ref[:count, :]
            pre = []
            for side in range(2):
                low = lax.dot_general(
                    group,
                    picks_all_ref[side * picks : (side + 1) * picks, :, :width].reshape(
                        cat_rows, width
                    ),
                    minor,
                    preferred_element_type=jnp.float32,
                )
                pre.append(
                    base[side]
                    + jnp.dot(spread(low), active_factor_ref[side], preferred_element_type=jnp.float32)
                )
            hidden = (jax.nn.gelu(pre[0], approximate=True) * pre[1]).astype(kind)
            low = lax.dot_general(
                hidden, active_factor_ref[2], minor, preferred_element_type=jnp.float32
            )
            low_spread = spread(low)
            part = jnp.dot(hidden, down_ref[...], preferred_element_type=jnp.float32)
            part = part + jnp.concatenate(
                [
                    jnp.dot(
                        low_spread,
                        jnp.concatenate(
                            [
                                picks_all_ref[k, :, width:]
                                for k in range(side, rank_pairs, 2)
                            ],
                            axis=0,
                        ),
                        preferred_element_type=jnp.float32,
                    )
                    for side in range(2)
                ],
                axis=1,
            )
            part = part.astype(kind)
            for place, slot in enumerate(slots):
                part_ref[slot] = part[place * rows : (place + 1) * rows, :]
            for key in keys:
                push(sib_copy(*key))

        def pair_sum(stream, way, far):
            sib_copy(stream, way, far).wait_recv()
            own = part_ref[0, stream, way, far].astype(jnp.float32)
            return own + sib_ref[stream, way, far].astype(jnp.float32)

        def ring_copy(stream, way, far):
            return remote(
                leave_ref.at[stream, way, far - 1],
                arrive_ref.at[stream, way, far - 1],
                sum_ring_send.at[stream, way, far - 1],
                sum_ring_recv.at[stream, way, far - 1],
                blk_ahead[way],
            )

        def arrived(stream, way, far):
            ring_copy(stream, way, far + 1).wait_recv()
            return arrive_ref[stream, way, far].astype(jnp.float32)

        totals = {}

        def pass_on(far):
            for stream, way, _ in keys_at(far):
                total = pair_sum(stream, way, far)
                if far == 0:
                    total = total + arrived(stream, FWD, 0) + arrived(stream, BWD, 0)
                    if stream == OTHER:
                        cross_out_ref[...] = total.astype(kind)
                        push(remote(cross_out_ref, cross_in_ref, sum_across_send, sum_across_recv, blk_across))
                    else:
                        totals[stream] = total
                    continue
                if far < reach(stream, way):
                    total = total + arrived(stream, way, far)
                leave_ref[stream, way, far - 1] = total.astype(kind)
                push(ring_copy(stream, way, far))

        for keep in keeps:
            keep.wait()
        for place in range(picks):
            number = active_ref[place]
            slab = factor_all_ref[number // kept, lax.rem(number, kept)].astype(jnp.float32)
            spare = jnp.zeros((factor_rows, 256 - hidden_dev), jnp.float32)
            slab = jnp.concatenate([slab, spare], axis=1)
            spots = pl.ds(place, factor_rows, stride=picks)
            wide_low_ref[spots, :] = slab[:, :128]
            wide_high_ref[spots, :] = slab[:, 128:]
        wide = jnp.concatenate([wide_low_ref[...], wide_high_ref[...]], axis=1)[:, :hidden_dev]
        active_factor_ref[...] = wide.astype(kind).reshape(active_factor_ref.shape)
        settle(ROWS)
        first_base = base_of(4)
        relay(PICKS, OTHER, 4)
        settle(PICKS)
        compute(4, first_base)
        for far in range(3, -1, -1):
            compute(far, base_of(far))
            pass_on(far + 1)
        pass_on(0)
        remote(cross_out_ref, cross_in_ref, sum_across_send, sum_across_recv, blk_across).wait_recv()
        total = totals[OWN] + cross_in_ref[...].astype(jnp.float32)
        out_ref[...] = (stream_ref[...].astype(jnp.float32) + total).astype(kind)
        for copy in sent:
            copy.wait_send()

    dma = pltpu.SemaphoreType.DMA
    block = (rows, width)
    vmem = pl.BlockSpec(memory_space=pltpu.VMEM)
    return pl.pallas_call(
        kernel,
        out_shape=jax.ShapeDtypeStruct(block, kind),
        in_specs=[vmem] * 7 + [pl.BlockSpec(memory_space=pltpu.SMEM)] + [vmem] * 2,
        out_specs=vmem,
        scratch_shapes=[
            pltpu.VMEM((rows, packed_width), kind),
            pltpu.VMEM((kept, catalog_width), kind),
            pltpu.VMEM((blocks, rows, packed_width), kind),
            pltpu.VMEM((blocks, picks, catalog_width), kind),
            pltpu.VMEM((holders,) + factors.shape, kind),
            pltpu.VMEM((holders, kept, catalog_width), kind),
            pltpu.VMEM((picks, catalog_width), kind),
            pltpu.VMEM((picks * factor_rows, 128), jnp.float32),
            pltpu.VMEM((picks * factor_rows, 128), jnp.float32),
            pltpu.VMEM((3, cat_rows, hidden_dev), kind),
            pltpu.VMEM((8 * rows, width), kind),
            pltpu.VMEM((2, 2, 2, 5) + block, kind),
            pltpu.VMEM((2, 2, 5) + block, kind),
            pltpu.VMEM((2, 2, 4) + block, kind),
            pltpu.VMEM((2, 2, 4) + block, kind),
            pltpu.VMEM(block, kind),
            pltpu.VMEM(block, kind),
            dma((3, 2, 2, 4)),
            dma((3, 2, 2, 4)),
            dma((3,)),
            dma((3,)),
            dma((2, 2, 2, 5)),
            dma((2, 2, 2, 5)),
            dma((holders - 1,)),
            dma((holders - 1,)),
            dma((4,)),
            dma((2, 2, 4)),
            dma((2, 2, 4)),
            dma,
            dma,
            dma((2, 2, 5)),
            dma((2, 2, 5)),
        ],
        compiler_params=pltpu.CompilerParams(collective_id=1, has_side_effects=True),
        name="sublayer",
    )(
        stream_rows,
        gain,
        slots,
        gate_in,
        down_out,
        active_rows,
        factors,
        active,
        gate_up,
        down,
    )


def local(
    stream,
    prenorm_gain,
    gate_up_weight,
    down_weight,
    adapter_gate_input,
    adapter_gate_output,
    adapter_down_input,
    adapter_down_output,
    adapter_of_request,
    request_of_slot,
):
    width = stream.shape[1]
    tok_rows = stream.shape[0]
    hidden_dev = down_weight.shape[0]
    rank_columns = adapter_down_output.shape[1]
    holders = lax.axis_size("adp")
    kept_rows = adapter_gate_input.shape[0]
    catalog = jnp.arange(kept_rows * holders, dtype=jnp.int32)
    used = jnp.any(adapter_of_request[:, None] == catalog[None, :], axis=0)
    order = jnp.cumsum(used.astype(jnp.int32)) - 1
    active_pos = jnp.arange(ACTIVE, dtype=jnp.int32)
    picked = used[None, :] & (order[None, :] == active_pos[:, None])
    active = jnp.sum(jnp.where(picked, catalog[None, :], 0), axis=1)
    table = jnp.arange(adapter_of_request.shape[0], dtype=jnp.int32)
    own_adapter = jnp.sum(
        jnp.where(request_of_slot[:, None] == table[None, :], adapter_of_request[None, :], 0),
        axis=1,
    )
    own_match = own_adapter[:, None] == active[None, :]
    own_slot = jnp.sum(jnp.where(own_match, active_pos[None, :], 0), axis=1)
    own_factors = jnp.concatenate(
        [
            adapter_gate_output.reshape(kept_rows, 2 * rank_columns, hidden_dev),
            adapter_down_input.transpose(0, 2, 1),
        ],
        axis=1,
    )
    slots = jnp.broadcast_to(own_slot.astype(jnp.bfloat16)[:, None], (tok_rows, 128))
    active_rows = jnp.broadcast_to(active.astype(jnp.float32)[:, None], (ACTIVE, 128))
    return sublayer(
        stream,
        prenorm_gain[None, :],
        slots,
        adapter_gate_input,
        adapter_down_output,
        active_rows,
        own_factors,
        active,
        gate_up_weight,
        down_weight,
        holders,
    )


def solution(mesh):
    in_specs = (
        P(("blk", "adp"), None),
        P(),
        P(None, "blk", None),
        P("blk", None),
        P("adp", None, None),
        P("adp", None, None, "blk"),
        P("adp", "blk", None),
        P("adp", None, None),
        P(),
        P(("blk", "adp")),
    )
    out_specs = P(("blk", "adp"), None)
    return jax.shard_map(local, mesh=mesh, in_specs=in_specs, out_specs=out_specs, check_vma=False)
```

```python
import jax
import jax.numpy as jnp
from jax import lax
from jax.experimental import pallas as pl
from jax.experimental.pallas import tpu as pltpu
from jax.sharding import PartitionSpec as P

ACTIVE = 16
RING = 8
FWD, BWD = 0, 1
OWN, OTHER = 0, 1

norm_eps = 1e-06


def normalize(rows, gain):
    value_rows = rows.astype(jnp.float32)
    scale = lax.rsqrt(jnp.mean(value_rows * value_rows, axis=-1, keepdims=True) + norm_eps)
    return (value_rows * scale * gain).astype(jnp.bfloat16)


def blk_index(x_hi, z, core):
    return x_hi * (2 * RING) + z * 2 + core


def greet(targets):
    barrier = pltpu.get_barrier_semaphore()
    for target in targets:
        pl.semaphore_signal(
            barrier, inc=1, device_id=target, device_id_type=pl.DeviceIdType.MESH
        )


def remote(src, dst, send_sem, recv_sem, target):
    return pltpu.make_async_remote_copy(
        src_ref=src,
        dst_ref=dst,
        send_sem=send_sem,
        recv_sem=recv_sem,
        device_id=target,
        device_id_type=pl.DeviceIdType.MESH,
    )


def reach(stream, way):
    return 4 if (stream == OWN) == (way == FWD) else 3


ROWS, PICKS, FACTORS = 0, 1, 2


def sublayer(
    stream_rows,
    gain,
    numbers,
    gate_in,
    down_out,
    factors,
    active,
    gate_up,
    down,
    holders,
):
    blocks = 4 * RING
    kept = gate_in.shape[0]
    rows, width = stream_rows.shape
    packed_width = width + numbers.shape[1]
    catalog_width = width + width // 2
    chunk = catalog_width // 6
    picks = numbers.shape[0] - rows
    factor_rows, hidden_dev = factors.shape[1:]
    cat_rows = picks * factor_rows // 3
    rank_pairs = blocks
    kind = stream_rows.dtype
    half = width // 2
    minor = (((1,), (1,)), ((), ()))

    def kernel(
        stream_ref,
        gain_ref,
        numbers_ref,
        gate_in_ref,
        down_out_ref,
        factor_ref,
        active_ref,
        gate_up_ref,
        down_ref,
        out_ref,
        own_ref,
        catalog_own_ref,
        all_ref,
        picks_all_ref,
        factor_all_ref,
        catalog_ref,
        picks_ref,
        wide_low_ref,
        wide_high_ref,
        active_factor_ref,
        group_ref,
        part_ref,
        sib_ref,
        leave_ref,
        arrive_ref,
        cross_out_ref,
        cross_in_ref,
        ring_send,
        ring_recv,
        across_send,
        across_recv,
        sib_send,
        sib_recv,
        catalog_send,
        catalog_recv,
        local_sem,
        sum_ring_send,
        sum_ring_recv,
        sum_across_send,
        sum_across_recv,
        sum_sib_send,
        sum_sib_recv,
    ):
        me = lax.axis_index("blk")
        me_adp = lax.axis_index("adp")
        x_hi = me // (2 * RING)
        z = lax.rem(me // 2, RING)
        core = lax.rem(me, 2)
        x_lo = lax.rem(me_adp, 2)
        y = me_adp // 2
        sibling = {"blk": blk_index(x_hi, z, 1 - core)}
        blk_across = {"blk": blk_index(1 - x_hi, z, core)}
        blk_ahead = {
            FWD: {"blk": blk_index(x_hi, lax.rem(z + 1, RING), core)},
            BWD: {"blk": blk_index(x_hi, lax.rem(z + RING - 1, RING), core)},
        }
        adp_across = {"adp": y * 2 + 1 - x_lo}
        adp_ahead = {
            FWD: {"adp": lax.rem(y + 1, RING) * 2 + x_lo},
            BWD: {"adp": lax.rem(y + RING - 1, RING) * 2 + x_lo},
        }
        adp_peers = [{"adp": lax.rem(me_adp + step, holders)} for step in range(1, holders)]
        across = [blk_across, blk_across, adp_across]
        ahead = [blk_ahead, blk_ahead, adp_ahead]
        source = [own_ref, picks_ref, factor_ref]
        landing = [all_ref, picks_all_ref, factor_all_ref]
        greeted = [sibling, blk_across, blk_ahead[FWD], blk_ahead[BWD]] + adp_peers
        greet(greeted)

        def pick_row(table, at_row):
            place = lax.broadcasted_iota(jnp.int32, table.shape, 0)
            kept_row = jnp.where(place == at_row, table.astype(jnp.float32), 0.0)
            return jnp.sum(kept_row, axis=0, keepdims=True)

        out_rows = [pick_row(down_out_ref[row], me // 2) for row in range(kept)]
        in_rows = [pick_row(gate_in_ref[row], me) for row in range(kept)]
        in_rows = jnp.concatenate(in_rows, axis=0)
        out_rows = jnp.concatenate(out_rows, axis=0)
        catalog_own_ref[:, :width] = in_rows.astype(kind)
        catalog_own_ref[:, width:] = jnp.where(
            core == 0, out_rows[:, :half], out_rows[:, half:]
        ).astype(kind)
        own_ref[:, :width] = normalize(stream_ref[...], gain_ref[...])
        own_ref[:, width:] = numbers_ref[:rows, :].astype(kind)
        pl.semaphore_wait(pltpu.get_barrier_semaphore(), len(greeted))
        sent = []

        def around(at, way, far):
            return lax.rem(at + RING - far, RING) if way == FWD else lax.rem(at + far, RING)

        def index_of(kind, stream, way, far, owner_core):
            if kind == FACTORS:
                return around(y, way, far) * 2 + (x_lo if stream == OWN else 1 - x_lo)
            x_of = x_hi if stream == OWN else 1 - x_hi
            return blk_index(x_of, around(z, way, far), owner_core)

        def push(copy):
            copy.start()
            sent.append(copy)

        def to_ring(src, index, kind, stream, way, far):
            push(
                remote(
                    src,
                    landing[kind].at[index],
                    ring_send.at[kind, stream, way, far],
                    ring_recv.at[kind, stream, way, far],
                    ahead[kind][way],
                )
            )

        def to_sibling(src, index, kind, stream, way, far):
            if kind == FACTORS:
                return
            push(
                remote(
                    src,
                    landing[kind].at[index],
                    sib_send.at[kind, stream, way, far],
                    sib_recv.at[kind, stream, way, far],
                    sibling,
                )
            )

        def launch(kind):
            index = index_of(kind, OWN, FWD, 0, core)
            src = source[kind]
            push(
                remote(
                    src,
                    landing[kind].at[index],
                    across_send.at[kind],
                    across_recv.at[kind],
                    across[kind],
                )
            )
            to_ring(src, index, kind, OWN, FWD, 0)
            to_ring(src, index, kind, OWN, BWD, 0)
            to_sibling(src, index, kind, OWN, FWD, 0)
            keep = pltpu.make_async_copy(src, landing[kind].at[index], local_sem.at[kind])
            keep.start()
            return keep

        def join(kind):
            index = index_of(kind, OTHER, FWD, 0, core)
            slab = landing[kind].at[index]
            remote(
                slab, slab, across_send.at[kind], across_recv.at[kind], across[kind]
            ).wait_recv()
            to_ring(slab, index, kind, OTHER, FWD, 0)
            to_ring(slab, index, kind, OTHER, BWD, 0)
            to_sibling(slab, index, kind, OTHER, FWD, 0)

        def relay(kind, stream, far):
            for way in (FWD, BWD):
                last = reach(stream, way)
                if far > last:
                    continue
                index = index_of(kind, stream, way, far, core)
                slab = landing[kind].at[index]
                remote(
                    slab,
                    slab,
                    ring_send.at[kind, stream, way, far - 1],
                    ring_recv.at[kind, stream, way, far - 1],
                    ahead[kind][way],
                ).wait_recv()
                if far < last:
                    to_ring(slab, index, kind, stream, way, far)
                to_sibling(slab, index, kind, stream, way, far)

        keeps = []
        for step, target in enumerate(adp_peers):
            copy = remote(
                catalog_own_ref,
                catalog_ref.at[me_adp],
                catalog_send.at[step],
                catalog_recv.at[step],
                target,
            )
            push(copy)
        keeps.append(launch(ROWS))
        keep = pltpu.make_async_copy(catalog_own_ref, catalog_ref.at[me_adp], local_sem.at[3])
        keep.start()
        relay(ROWS, OWN, 1)
        join(ROWS)
        relay(ROWS, OWN, 2)

        for step, target in enumerate(adp_peers):
            slab = catalog_ref.at[lax.rem(me_adp + holders - step - 1, holders)]
            remote(
                slab, slab, catalog_send.at[step], catalog_recv.at[step], target
            ).wait_recv()
        keep.wait()
        keeps.append(launch(FACTORS))
        for part in range(6):
            cols = slice(part * chunk, (part + 1) * chunk)
            total = jnp.zeros((picks, chunk), jnp.float32)
            for holder in range(holders):
                held = catalog_ref[holder, :, cols].astype(jnp.float32)
                for row in range(kept):
                    number = float(holder * kept + row)
                    mask = jnp.where(numbers_ref[rows:, :] == number, 1.0, 0.0)
                    mask = jnp.concatenate([mask] * (chunk // 128), axis=1)
                    total = total + mask * held[row : row + 1, :]
            picks_ref[:, cols] = total.astype(picks_ref.dtype)

        keeps.append(launch(PICKS))
        relay(ROWS, OTHER, 1)
        join(FACTORS)
        relay(FACTORS, OWN, 1)
        relay(ROWS, OWN, 3)
        relay(ROWS, OTHER, 2)
        relay(PICKS, OWN, 1)
        join(PICKS)
        relay(FACTORS, OTHER, 1)
        relay(FACTORS, OWN, 2)
        relay(ROWS, OTHER, 3)
        relay(ROWS, OWN, 4)
        relay(PICKS, OWN, 2)
        relay(PICKS, OTHER, 1)
        relay(FACTORS, OTHER, 2)
        relay(FACTORS, OWN, 3)
        relay(ROWS, OTHER, 4)
        relay(PICKS, OWN, 3)
        relay(PICKS, OTHER, 2)
        relay(FACTORS, OTHER, 3)
        relay(FACTORS, OWN, 4)
        relay(PICKS, OTHER, 3)
        relay(PICKS, OWN, 4)
        relay(FACTORS, OTHER, 4)
        def at(stream, way, far, owner_core):
            x_of = x_hi if stream == OWN else 1 - x_hi
            z_of = lax.rem(z + far, RING) if way == FWD else lax.rem(z + RING - far, RING)
            return blk_index(x_of, z_of, owner_core)

        def settle(slabs):
            for far in range(0, 5):
                for stream in (OWN, OTHER):
                    for way in (FWD, BWD):
                        if far > reach(stream, way) or (far == 0 and way == BWD):
                            continue
                        slab = landing[slabs].at[index_of(slabs, stream, way, far, 1 - core)]
                        remote(
                            slab,
                            slab,
                            sib_send.at[slabs, stream, way, far],
                            sib_recv.at[slabs, stream, way, far],
                            sibling,
                        ).wait_recv()

        def keys_at(far):
            return [
                (stream, way, far)
                for stream in (OTHER, OWN)
                for way in (FWD, BWD)
                if far <= reach(stream, way) and not (far == 0 and way == BWD)
            ]

        def sib_copy(stream, way, far):
            return remote(
                part_ref.at[1, stream, way, far],
                sib_ref.at[stream, way, far],
                sum_sib_send.at[stream, way, far],
                sum_sib_recv.at[stream, way, far],
                sibling,
            )

        def slots_at(far):
            return [(side,) + key for side in (1, 0) for key in keys_at(far)]

        def base_of(far):
            slots = slots_at(far)
            for place, (side, stream, way, _) in enumerate(slots):
                index = at(stream, way, far, core if side == 0 else 1 - core)
                group_ref[place * rows : (place + 1) * rows, :] = all_ref[index, :, :width]
            group = group_ref[: len(slots) * rows, :]
            return [
                lax.dot_general(
                    group, gate_up_ref[side], minor, preferred_element_type=jnp.float32
                )
                for side in range(2)
            ]

        def compute(far, base):
            keys = keys_at(far)
            slots = slots_at(far)
            count = len(slots) * rows
            numbers = []
            for place, (side, stream, way, _) in enumerate(slots):
                index = at(stream, way, far, core if side == 0 else 1 - core)
                numbers.append(all_ref[index, :, width:].astype(jnp.float32))
            number = jnp.concatenate(numbers, axis=0)
            number = jnp.concatenate([number] * (cat_rows // number.shape[1]), axis=1)
            lane = lax.broadcasted_iota(jnp.int32, (count, cat_rows), 1)
            match = number == lax.rem(lane, ACTIVE).astype(jnp.float32)

            def spread(low):
                return jnp.where(match, low, 0.0).astype(kind)

            group = group_ref[:count, :]
            pre = []
            for side in range(2):
                low = lax.dot_general(
                    group,
                    picks_all_ref[side * picks : (side + 1) * picks, :, :width].reshape(
                        cat_rows, width
                    ),
                    minor,
                    preferred_element_type=jnp.float32,
                )
                pre.append(
                    base[side]
                    + jnp.dot(spread(low), active_factor_ref[side], preferred_element_type=jnp.float32)
                )
            hidden = (jax.nn.gelu(pre[0], approximate=True) * pre[1]).astype(kind)
            low = lax.dot_general(
                hidden, active_factor_ref[2], minor, preferred_element_type=jnp.float32
            )
            low_spread = spread(low)
            part = jnp.dot(hidden, down_ref[...], preferred_element_type=jnp.float32)
            part = part + jnp.concatenate(
                [
                    jnp.dot(
                        low_spread,
                        jnp.concatenate(
                            [
                                picks_all_ref[k, :, width:]
                                for k in range(side, rank_pairs, 2)
                            ],
                            axis=0,
                        ),
                        preferred_element_type=jnp.float32,
                    )
                    for side in range(2)
                ],
                axis=1,
            )
            part = part.astype(kind)
            for place, slot in enumerate(slots):
                part_ref[slot] = part[place * rows : (place + 1) * rows, :]
            for key in keys:
                push(sib_copy(*key))

        def pair_sum(stream, way, far):
            sib_copy(stream, way, far).wait_recv()
            own = part_ref[0, stream, way, far].astype(jnp.float32)
            return own + sib_ref[stream, way, far].astype(jnp.float32)

        def ring_copy(stream, way, far):
            return remote(
                leave_ref.at[stream, way, far - 1],
                arrive_ref.at[stream, way, far - 1],
                sum_ring_send.at[stream, way, far - 1],
                sum_ring_recv.at[stream, way, far - 1],
                blk_ahead[way],
            )

        def arrived(stream, way, far):
            ring_copy(stream, way, far + 1).wait_recv()
            return arrive_ref[stream, way, far].astype(jnp.float32)

        totals = {}

        def pass_on(far):
            for stream, way, _ in keys_at(far):
                total = pair_sum(stream, way, far)
                if far == 0:
                    total = total + arrived(stream, FWD, 0) + arrived(stream, BWD, 0)
                    if stream == OTHER:
                        cross_out_ref[...] = total.astype(kind)
                        push(remote(cross_out_ref, cross_in_ref, sum_across_send, sum_across_recv, blk_across))
                    else:
                        totals[stream] = total
                    continue
                if far < reach(stream, way):
                    total = total + arrived(stream, way, far)
                leave_ref[stream, way, far - 1] = total.astype(kind)
                push(ring_copy(stream, way, far))

        for keep in keeps:
            keep.wait()
        for place in range(picks):
            number = active_ref[place]
            slab = factor_all_ref[number // kept, lax.rem(number, kept)].astype(jnp.float32)
            spare = jnp.zeros((factor_rows, 256 - hidden_dev), jnp.float32)
            slab = jnp.concatenate([slab, spare], axis=1)
            spots = pl.ds(place, factor_rows, stride=picks)
            wide_low_ref[spots, :] = slab[:, :128]
            wide_high_ref[spots, :] = slab[:, 128:]
        wide = jnp.concatenate([wide_low_ref[...], wide_high_ref[...]], axis=1)[:, :hidden_dev]
        active_factor_ref[...] = wide.astype(kind).reshape(active_factor_ref.shape)
        settle(ROWS)
        first_base = base_of(4)
        relay(PICKS, OTHER, 4)
        settle(PICKS)
        compute(4, first_base)
        for far in range(3, -1, -1):
            base = base_of(far)
            pass_on(far + 1)
            compute(far, base)
        pass_on(0)
        remote(cross_out_ref, cross_in_ref, sum_across_send, sum_across_recv, blk_across).wait_recv()
        total = totals[OWN] + cross_in_ref[...].astype(jnp.float32)
        out_ref[...] = (stream_ref[...].astype(jnp.float32) + total).astype(kind)
        for copy in sent:
            copy.wait_send()

    dma = pltpu.SemaphoreType.DMA
    block = (rows, width)
    vmem = pl.BlockSpec(memory_space=pltpu.VMEM)
    return pl.pallas_call(
        kernel,
        out_shape=jax.ShapeDtypeStruct(block, kind),
        in_specs=[vmem] * 6 + [pl.BlockSpec(memory_space=pltpu.SMEM)] + [vmem] * 2,
        out_specs=vmem,
        scratch_shapes=[
            pltpu.VMEM((rows, packed_width), kind),
            pltpu.VMEM((kept, catalog_width), kind),
            pltpu.VMEM((blocks, rows, packed_width), kind),
            pltpu.VMEM((blocks, picks, catalog_width), kind),
            pltpu.VMEM((holders,) + factors.shape, kind),
            pltpu.VMEM((holders, kept, catalog_width), kind),
            pltpu.VMEM((picks, catalog_width), kind),
            pltpu.VMEM((picks * factor_rows, 128), jnp.float32),
            pltpu.VMEM((picks * factor_rows, 128), jnp.float32),
            pltpu.VMEM((3, cat_rows, hidden_dev), kind),
            pltpu.VMEM((8 * rows, width), kind),
            pltpu.VMEM((2, 2, 2, 5) + block, kind),
            pltpu.VMEM((2, 2, 5) + block, kind),
            pltpu.VMEM((2, 2, 4) + block, kind),
            pltpu.VMEM((2, 2, 4) + block, kind),
            pltpu.VMEM(block, kind),
            pltpu.VMEM(block, kind),
            dma((3, 2, 2, 4)),
            dma((3, 2, 2, 4)),
            dma((3,)),
            dma((3,)),
            dma((2, 2, 2, 5)),
            dma((2, 2, 2, 5)),
            dma((holders - 1,)),
            dma((holders - 1,)),
            dma((4,)),
            dma((2, 2, 4)),
            dma((2, 2, 4)),
            dma,
            dma,
            dma((2, 2, 5)),
            dma((2, 2, 5)),
        ],
        compiler_params=pltpu.CompilerParams(collective_id=1, has_side_effects=True),
        name="sublayer",
    )(
        stream_rows,
        gain,
        numbers,
        gate_in,
        down_out,
        factors,
        active,
        gate_up,
        down,
    )


def local(
    stream,
    prenorm_gain,
    gate_up_weight,
    down_weight,
    adapter_gate_input,
    adapter_gate_output,
    adapter_down_input,
    adapter_down_output,
    adapter_of_request,
    request_of_slot,
):
    width = stream.shape[1]
    tok_rows = stream.shape[0]
    hidden_dev = down_weight.shape[0]
    rank_columns = adapter_down_output.shape[1]
    holders = lax.axis_size("adp")
    kept_rows = adapter_gate_input.shape[0]
    catalog = jnp.arange(kept_rows * holders, dtype=jnp.int32)
    used = jnp.any(adapter_of_request[:, None] == catalog[None, :], axis=0)
    order = jnp.cumsum(used.astype(jnp.int32)) - 1
    active_pos = jnp.arange(ACTIVE, dtype=jnp.int32)
    picked = used[None, :] & (order[None, :] == active_pos[:, None])
    active = jnp.sum(jnp.where(picked, catalog[None, :], 0), axis=1)
    table = jnp.arange(adapter_of_request.shape[0], dtype=jnp.int32)
    own_adapter = jnp.sum(
        jnp.where(request_of_slot[:, None] == table[None, :], adapter_of_request[None, :], 0),
        axis=1,
    )
    own_match = own_adapter[:, None] == active[None, :]
    own_slot = jnp.sum(jnp.where(own_match, active_pos[None, :], 0), axis=1)
    own_factors = jnp.concatenate(
        [
            adapter_gate_output.reshape(kept_rows, 2 * rank_columns, hidden_dev),
            adapter_down_input.transpose(0, 2, 1),
        ],
        axis=1,
    )
    numbers = jnp.concatenate([own_slot, active]).astype(jnp.float32)
    numbers = jnp.broadcast_to(numbers[:, None], (tok_rows + ACTIVE, 128))
    return sublayer(
        stream,
        prenorm_gain,
        numbers,
        adapter_gate_input,
        adapter_down_output,
        own_factors,
        active,
        gate_up_weight,
        down_weight,
        holders,
    )


def solution(mesh):
    in_specs = (
        P(("blk", "adp"), None),
        P(),
        P(None, "blk", None),
        P("blk", None),
        P("adp", None, None),
        P("adp", None, None, "blk"),
        P("adp", "blk", None),
        P("adp", None, None),
        P(),
        P(("blk", "adp")),
    )
    out_specs = P(("blk", "adp"), None)
    return jax.shard_map(local, mesh=mesh, in_specs=in_specs, out_specs=out_specs, check_vma=False)
```

```python
import jax
import jax.numpy as jnp
from jax import lax
from jax.experimental import pallas as pl
from jax.experimental.pallas import tpu as pltpu
from jax.sharding import PartitionSpec as P

ACTIVE = 16
RING = 8
FWD, BWD = 0, 1
OWN, OTHER = 0, 1

norm_eps = 1e-06


def normalize(rows, gain):
    value_rows = rows.astype(jnp.float32)
    scale = lax.rsqrt(jnp.mean(value_rows * value_rows, axis=-1, keepdims=True) + norm_eps)
    return (value_rows * scale * gain).astype(jnp.bfloat16)


def blk_index(x_hi, z, core):
    return x_hi * (2 * RING) + z * 2 + core


def greet(targets):
    barrier = pltpu.get_barrier_semaphore()
    for target in targets:
        pl.semaphore_signal(
            barrier, inc=1, device_id=target, device_id_type=pl.DeviceIdType.MESH
        )


def remote(src, dst, send_sem, recv_sem, target):
    return pltpu.make_async_remote_copy(
        src_ref=src,
        dst_ref=dst,
        send_sem=send_sem,
        recv_sem=recv_sem,
        device_id=target,
        device_id_type=pl.DeviceIdType.MESH,
    )


def reach(stream, way):
    return 4 if (stream == OWN) == (way == FWD) else 3


ROWS, PICKS, FACTORS = 0, 1, 2


def sublayer(
    stream_rows,
    gain,
    numbers,
    gate_in,
    down_out,
    factors,
    active,
    gate_up,
    down,
    holders,
):
    blocks = 4 * RING
    kept = gate_in.shape[0]
    rows, width = stream_rows.shape
    packed_width = width + numbers.shape[1]
    catalog_width = width + width // 2
    chunk = catalog_width // 6
    picks = numbers.shape[0] - rows
    factor_rows, hidden_dev = factors.shape[1:]
    cat_rows = picks * factor_rows // 3
    rank_pairs = blocks
    kind = stream_rows.dtype
    half = width // 2
    minor = (((1,), (1,)), ((), ()))

    def kernel(
        stream_ref,
        gain_ref,
        numbers_ref,
        gate_in_ref,
        down_out_ref,
        factor_ref,
        active_ref,
        gate_up_ref,
        down_ref,
        out_ref,
        own_ref,
        catalog_own_ref,
        all_ref,
        picks_all_ref,
        factor_all_ref,
        catalog_ref,
        picks_ref,
        wide_low_ref,
        wide_high_ref,
        active_factor_ref,
        group_ref,
        part_ref,
        sib_ref,
        leave_ref,
        arrive_ref,
        cross_out_ref,
        cross_in_ref,
        ring_send,
        ring_recv,
        across_send,
        across_recv,
        sib_send,
        sib_recv,
        catalog_send,
        catalog_recv,
        local_sem,
        sum_ring_send,
        sum_ring_recv,
        sum_across_send,
        sum_across_recv,
        sum_sib_send,
        sum_sib_recv,
    ):
        me = lax.axis_index("blk")
        me_adp = lax.axis_index("adp")
        x_hi = me // (2 * RING)
        z = lax.rem(me // 2, RING)
        core = lax.rem(me, 2)
        x_lo = lax.rem(me_adp, 2)
        y = me_adp // 2
        sibling = {"blk": blk_index(x_hi, z, 1 - core)}
        blk_across = {"blk": blk_index(1 - x_hi, z, core)}
        blk_ahead = {
            FWD: {"blk": blk_index(x_hi, lax.rem(z + 1, RING), core)},
            BWD: {"blk": blk_index(x_hi, lax.rem(z + RING - 1, RING), core)},
        }
        adp_across = {"adp": y * 2 + 1 - x_lo}
        adp_ahead = {
            FWD: {"adp": lax.rem(y + 1, RING) * 2 + x_lo},
            BWD: {"adp": lax.rem(y + RING - 1, RING) * 2 + x_lo},
        }
        adp_peers = [{"adp": lax.rem(me_adp + step, holders)} for step in range(1, holders)]
        across = [blk_across, blk_across, adp_across]
        ahead = [blk_ahead, blk_ahead, adp_ahead]
        source = [own_ref, picks_ref, factor_ref]
        landing = [all_ref, picks_all_ref, factor_all_ref]
        greeted = [sibling, blk_across, blk_ahead[FWD], blk_ahead[BWD]] + adp_peers
        greet(greeted)

        def pick_row(table, at_row):
            place = lax.broadcasted_iota(jnp.int32, table.shape, 0)
            kept_row = jnp.where(place == at_row, table.astype(jnp.float32), 0.0)
            return jnp.sum(kept_row, axis=0, keepdims=True)

        out_rows = [pick_row(down_out_ref[row], me // 2) for row in range(kept)]
        in_rows = [pick_row(gate_in_ref[row], me) for row in range(kept)]
        in_rows = jnp.concatenate(in_rows, axis=0)
        out_rows = jnp.concatenate(out_rows, axis=0)
        catalog_own_ref[:, :width] = in_rows.astype(kind)
        catalog_own_ref[:, width:] = jnp.where(
            core == 0, out_rows[:, :half], out_rows[:, half:]
        ).astype(kind)
        own_ref[:, :width] = normalize(stream_ref[...], gain_ref[...])
        own_ref[:, width:] = numbers_ref[:rows, :].astype(kind)
        pl.semaphore_wait(pltpu.get_barrier_semaphore(), len(greeted))
        sent = []

        def around(at, way, far):
            return lax.rem(at + RING - far, RING) if way == FWD else lax.rem(at + far, RING)

        def index_of(kind, stream, way, far, owner_core):
            if kind == FACTORS:
                return around(y, way, far) * 2 + (x_lo if stream == OWN else 1 - x_lo)
            x_of = x_hi if stream == OWN else 1 - x_hi
            return blk_index(x_of, around(z, way, far), owner_core)

        def push(copy):
            copy.start()
            sent.append(copy)

        def to_ring(src, index, kind, stream, way, far):
            push(
                remote(
                    src,
                    landing[kind].at[index],
                    ring_send.at[kind, stream, way, far],
                    ring_recv.at[kind, stream, way, far],
                    ahead[kind][way],
                )
            )

        def to_sibling(src, index, kind, stream, way, far):
            if kind == FACTORS:
                return
            push(
                remote(
                    src,
                    landing[kind].at[index],
                    sib_send.at[kind, stream, way, far],
                    sib_recv.at[kind, stream, way, far],
                    sibling,
                )
            )

        def launch(kind):
            index = index_of(kind, OWN, FWD, 0, core)
            src = source[kind]
            push(
                remote(
                    src,
                    landing[kind].at[index],
                    across_send.at[kind],
                    across_recv.at[kind],
                    across[kind],
                )
            )
            to_ring(src, index, kind, OWN, FWD, 0)
            to_ring(src, index, kind, OWN, BWD, 0)
            to_sibling(src, index, kind, OWN, FWD, 0)
            keep = pltpu.make_async_copy(src, landing[kind].at[index], local_sem.at[kind])
            keep.start()
            return keep

        def join(kind):
            index = index_of(kind, OTHER, FWD, 0, core)
            slab = landing[kind].at[index]
            remote(
                slab, slab, across_send.at[kind], across_recv.at[kind], across[kind]
            ).wait_recv()
            to_ring(slab, index, kind, OTHER, FWD, 0)
            to_ring(slab, index, kind, OTHER, BWD, 0)
            to_sibling(slab, index, kind, OTHER, FWD, 0)

        def relay(kind, stream, far):
            for way in (FWD, BWD):
                last = reach(stream, way)
                if far > last:
                    continue
                index = index_of(kind, stream, way, far, core)
                slab = landing[kind].at[index]
                remote(
                    slab,
                    slab,
                    ring_send.at[kind, stream, way, far - 1],
                    ring_recv.at[kind, stream, way, far - 1],
                    ahead[kind][way],
                ).wait_recv()
                if far < last:
                    to_ring(slab, index, kind, stream, way, far)
                to_sibling(slab, index, kind, stream, way, far)

        keeps = []
        for step, target in enumerate(adp_peers):
            copy = remote(
                catalog_own_ref,
                catalog_ref.at[me_adp],
                catalog_send.at[step],
                catalog_recv.at[step],
                target,
            )
            push(copy)
        keeps.append(launch(ROWS))
        keep = pltpu.make_async_copy(catalog_own_ref, catalog_ref.at[me_adp], local_sem.at[3])
        keep.start()
        relay(ROWS, OWN, 1)
        join(ROWS)
        relay(ROWS, OWN, 2)

        for step, target in enumerate(adp_peers):
            slab = catalog_ref.at[lax.rem(me_adp + holders - step - 1, holders)]
            remote(
                slab, slab, catalog_send.at[step], catalog_recv.at[step], target
            ).wait_recv()
        keep.wait()
        keeps.append(launch(FACTORS))
        for part in range(6):
            cols = slice(part * chunk, (part + 1) * chunk)
            total = jnp.zeros((picks, chunk), jnp.float32)
            for holder in range(holders):
                held = catalog_ref[holder, :, cols].astype(jnp.float32)
                for row in range(kept):
                    number = float(holder * kept + row)
                    mask = jnp.where(numbers_ref[rows:, :] == number, 1.0, 0.0)
                    mask = jnp.concatenate([mask] * (chunk // 128), axis=1)
                    total = total + mask * held[row : row + 1, :]
            picks_ref[:, cols] = total.astype(picks_ref.dtype)

        keeps.append(launch(PICKS))
        relay(ROWS, OTHER, 1)
        join(FACTORS)
        relay(FACTORS, OWN, 1)
        relay(ROWS, OWN, 3)
        relay(ROWS, OTHER, 2)
        relay(PICKS, OWN, 1)
        join(PICKS)
        relay(FACTORS, OTHER, 1)
        relay(FACTORS, OWN, 2)
        relay(ROWS, OTHER, 3)
        relay(ROWS, OWN, 4)
        relay(PICKS, OWN, 2)
        relay(PICKS, OTHER, 1)
        relay(FACTORS, OTHER, 2)
        relay(FACTORS, OWN, 3)
        relay(ROWS, OTHER, 4)
        relay(PICKS, OWN, 3)
        relay(PICKS, OTHER, 2)
        relay(FACTORS, OTHER, 3)
        relay(FACTORS, OWN, 4)
        relay(PICKS, OTHER, 3)
        relay(PICKS, OWN, 4)
        relay(FACTORS, OTHER, 4)
        def at(stream, way, far, owner_core):
            x_of = x_hi if stream == OWN else 1 - x_hi
            z_of = lax.rem(z + far, RING) if way == FWD else lax.rem(z + RING - far, RING)
            return blk_index(x_of, z_of, owner_core)

        def settle(slabs):
            for far in range(0, 5):
                for stream in (OWN, OTHER):
                    for way in (FWD, BWD):
                        if far > reach(stream, way) or (far == 0 and way == BWD):
                            continue
                        slab = landing[slabs].at[index_of(slabs, stream, way, far, 1 - core)]
                        remote(
                            slab,
                            slab,
                            sib_send.at[slabs, stream, way, far],
                            sib_recv.at[slabs, stream, way, far],
                            sibling,
                        ).wait_recv()

        def keys_at(far):
            return [
                (stream, way, far)
                for stream in (OTHER, OWN)
                for way in (FWD, BWD)
                if far <= reach(stream, way) and not (far == 0 and way == BWD)
            ]

        def sib_copy(stream, way, far):
            return remote(
                part_ref.at[1, stream, way, far],
                sib_ref.at[stream, way, far],
                sum_sib_send.at[stream, way, far],
                sum_sib_recv.at[stream, way, far],
                sibling,
            )

        def slots_at(far):
            return [(side,) + key for side in (1, 0) for key in keys_at(far)]

        def base_of(far):
            slots = slots_at(far)
            for place, (side, stream, way, _) in enumerate(slots):
                index = at(stream, way, far, core if side == 0 else 1 - core)
                group_ref[place * rows : (place + 1) * rows, :] = all_ref[index, :, :width]
            group = group_ref[: len(slots) * rows, :]
            return [
                lax.dot_general(
                    group, gate_up_ref[side], minor, preferred_element_type=jnp.float32
                )
                for side in range(2)
            ]

        def compute(far, base):
            keys = keys_at(far)
            slots = slots_at(far)
            count = len(slots) * rows
            numbers = []
            for place, (side, stream, way, _) in enumerate(slots):
                index = at(stream, way, far, core if side == 0 else 1 - core)
                numbers.append(all_ref[index, :, width:].astype(jnp.float32))
            number = jnp.concatenate(numbers, axis=0)
            number = jnp.concatenate([number] * (cat_rows // number.shape[1]), axis=1)
            lane = lax.broadcasted_iota(jnp.int32, (count, cat_rows), 1)
            match = number == lax.rem(lane, ACTIVE).astype(jnp.float32)

            def spread(low):
                return jnp.where(match, low, 0.0).astype(kind)

            group = group_ref[:count, :]
            pre = []
            for side in range(2):
                low = lax.dot_general(
                    group,
                    picks_all_ref[side * picks : (side + 1) * picks, :, :width].reshape(
                        cat_rows, width
                    ),
                    minor,
                    preferred_element_type=jnp.float32,
                )
                pre.append(
                    base[side]
                    + jnp.dot(spread(low), active_factor_ref[side], preferred_element_type=jnp.float32)
                )
            hidden = (jax.nn.gelu(pre[0], approximate=True) * pre[1]).astype(kind)
            low = lax.dot_general(
                hidden, active_factor_ref[2], minor, preferred_element_type=jnp.float32
            )
            low_spread = spread(low)
            part = jnp.dot(hidden, down_ref[...], preferred_element_type=jnp.float32)
            part = part + jnp.concatenate(
                [
                    jnp.dot(
                        low_spread,
                        jnp.concatenate(
                            [
                                picks_all_ref[k, :, width:]
                                for k in range(side, rank_pairs, 2)
                            ],
                            axis=0,
                        ),
                        preferred_element_type=jnp.float32,
                    )
                    for side in range(2)
                ],
                axis=1,
            )
            part = part.astype(kind)
            for place, slot in enumerate(slots):
                part_ref[slot] = part[place * rows : (place + 1) * rows, :]
            for key in keys:
                push(sib_copy(*key))

        def pair_sum(stream, way, far):
            sib_copy(stream, way, far).wait_recv()
            own = part_ref[0, stream, way, far].astype(jnp.float32)
            return own + sib_ref[stream, way, far].astype(jnp.float32)

        def ring_copy(stream, way, far):
            return remote(
                leave_ref.at[stream, way, far - 1],
                arrive_ref.at[stream, way, far - 1],
                sum_ring_send.at[stream, way, far - 1],
                sum_ring_recv.at[stream, way, far - 1],
                blk_ahead[way],
            )

        def arrived(stream, way, far):
            ring_copy(stream, way, far + 1).wait_recv()
            return arrive_ref[stream, way, far].astype(jnp.float32)

        totals = {}

        def pass_on(far):
            for stream, way, _ in keys_at(far):
                total = pair_sum(stream, way, far)
                if far == 0:
                    total = total + arrived(stream, FWD, 0) + arrived(stream, BWD, 0)
                    if stream == OTHER:
                        cross_out_ref[...] = total.astype(kind)
                        push(remote(cross_out_ref, cross_in_ref, sum_across_send, sum_across_recv, blk_across))
                    else:
                        totals[stream] = total
                    continue
                if far < reach(stream, way):
                    total = total + arrived(stream, way, far)
                leave_ref[stream, way, far - 1] = total.astype(kind)
                push(ring_copy(stream, way, far))

        for keep in keeps:
            keep.wait()
        for place in range(picks):
            number = active_ref[place]
            slab = factor_all_ref[number // kept, lax.rem(number, kept)].astype(jnp.float32)
            spare = jnp.zeros((factor_rows, 256 - hidden_dev), jnp.float32)
            slab = jnp.concatenate([slab, spare], axis=1)
            spots = pl.ds(place, factor_rows, stride=picks)
            wide_low_ref[spots, :] = slab[:, :128]
            wide_high_ref[spots, :] = slab[:, 128:]
        wide = jnp.concatenate([wide_low_ref[...], wide_high_ref[...]], axis=1)[:, :hidden_dev]
        active_factor_ref[...] = wide.astype(kind).reshape(active_factor_ref.shape)
        settle(ROWS)
        first_base = base_of(4)
        relay(PICKS, OTHER, 4)
        settle(PICKS)
        compute(4, first_base)
        for far in range(3, -1, -1):
            compute(far, base_of(far))
            pass_on(far + 1)
        pass_on(0)
        remote(cross_out_ref, cross_in_ref, sum_across_send, sum_across_recv, blk_across).wait_recv()
        total = totals[OWN] + cross_in_ref[...].astype(jnp.float32)
        out_ref[...] = (stream_ref[...].astype(jnp.float32) + total).astype(kind)
        for copy in sent:
            copy.wait_send()

    dma = pltpu.SemaphoreType.DMA
    block = (rows, width)
    vmem = pl.BlockSpec(memory_space=pltpu.VMEM)
    return pl.pallas_call(
        kernel,
        out_shape=jax.ShapeDtypeStruct(block, kind),
        in_specs=[vmem] * 6 + [pl.BlockSpec(memory_space=pltpu.SMEM)] + [vmem] * 2,
        out_specs=vmem,
        scratch_shapes=[
            pltpu.VMEM((rows, packed_width), kind),
            pltpu.VMEM((kept, catalog_width), kind),
            pltpu.VMEM((blocks, rows, packed_width), kind),
            pltpu.VMEM((blocks, picks, catalog_width), kind),
            pltpu.VMEM((holders,) + factors.shape, kind),
            pltpu.VMEM((holders, kept, catalog_width), kind),
            pltpu.VMEM((picks, catalog_width), kind),
            pltpu.VMEM((picks * factor_rows, 128), jnp.float32),
            pltpu.VMEM((picks * factor_rows, 128), jnp.float32),
            pltpu.VMEM((3, cat_rows, hidden_dev), kind),
            pltpu.VMEM((8 * rows, width), kind),
            pltpu.VMEM((2, 2, 2, 5) + block, kind),
            pltpu.VMEM((2, 2, 5) + block, kind),
            pltpu.VMEM((2, 2, 4) + block, kind),
            pltpu.VMEM((2, 2, 4) + block, kind),
            pltpu.VMEM(block, kind),
            pltpu.VMEM(block, kind),
            dma((3, 2, 2, 4)),
            dma((3, 2, 2, 4)),
            dma((3,)),
            dma((3,)),
            dma((2, 2, 2, 5)),
            dma((2, 2, 2, 5)),
            dma((holders - 1,)),
            dma((holders - 1,)),
            dma((4,)),
            dma((2, 2, 4)),
            dma((2, 2, 4)),
            dma,
            dma,
            dma((2, 2, 5)),
            dma((2, 2, 5)),
        ],
        compiler_params=pltpu.CompilerParams(collective_id=1, has_side_effects=True),
        name="sublayer",
    )(
        stream_rows,
        gain,
        numbers,
        gate_in,
        down_out,
        factors,
        active,
        gate_up,
        down,
    )


def local(
    stream,
    prenorm_gain,
    gate_up_weight,
    down_weight,
    adapter_gate_input,
    adapter_gate_output,
    adapter_down_input,
    adapter_down_output,
    adapter_of_request,
    request_of_slot,
):
    width = stream.shape[1]
    tok_rows = stream.shape[0]
    hidden_dev = down_weight.shape[0]
    rank_columns = adapter_down_output.shape[1]
    holders = lax.axis_size("adp")
    kept_rows = adapter_gate_input.shape[0]
    catalog = jnp.arange(kept_rows * holders, dtype=jnp.int32)
    used = jnp.any(adapter_of_request[:, None] == catalog[None, :], axis=0)
    order = jnp.cumsum(used.astype(jnp.int32)) - 1
    active_pos = jnp.arange(ACTIVE, dtype=jnp.int32)
    picked = used[None, :] & (order[None, :] == active_pos[:, None])
    active = jnp.sum(jnp.where(picked, catalog[None, :], 0), axis=1)
    table = jnp.arange(adapter_of_request.shape[0], dtype=jnp.int32)
    own_adapter = jnp.sum(
        jnp.where(request_of_slot[:, None] == table[None, :], adapter_of_request[None, :], 0),
        axis=1,
    )
    own_match = own_adapter[:, None] == active[None, :]
    own_slot = jnp.sum(jnp.where(own_match, active_pos[None, :], 0), axis=1)
    own_factors = jnp.concatenate(
        [
            adapter_gate_output.reshape(kept_rows, 2 * rank_columns, hidden_dev),
            adapter_down_input.transpose(0, 2, 1),
        ],
        axis=1,
    )
    numbers = jnp.concatenate([own_slot, active]).astype(jnp.float32)
    numbers = jnp.broadcast_to(numbers[:, None], (tok_rows + ACTIVE, 128))
    return sublayer(
        stream,
        prenorm_gain,
        numbers,
        adapter_gate_input,
        adapter_down_output,
        own_factors,
        active,
        gate_up_weight,
        down_weight,
        holders,
    )


def solution(mesh):
    in_specs = (
        P(("blk", "adp"), None),
        P(),
        P(None, "blk", None),
        P("blk", None),
        P("adp", None, None),
        P("adp", None, None, "blk"),
        P("adp", "blk", None),
        P("adp", None, None),
        P(),
        P(("blk", "adp")),
    )
    out_specs = P(("blk", "adp"), None)
    return jax.shard_map(local, mesh=mesh, in_specs=in_specs, out_specs=out_specs, check_vma=False)
```
